128 devices in a mesh: gx: 4 (over z), gy: 32 (over y, x, core).
Axes of the slice: x: 4, y: 4, z: 4, core: 2. Of those that a mesh axis runs over, the one named last changes fastest.
Arguments:
- densities: float32 [2048, 2, 128, 128], P(('gx', 'gy')), may hold values from -6 to 6
- hamiltonian: float32 [2, 128, 128], replicated, may hold values from -3 to 3, as said below
- couplings: float32 [4, 128, 128], replicated, may hold values from -1 to 1, as said below
- decay_rates: float32 [4], replicated, may hold values from 0.5 to 2
- correlation: float32 [2, 4], replicated, may hold values from 0.25 to 1.5
- upper_link: int32 [2048, 4], P(('gx', 'gy')), may hold values from 0 to 2048, as said below
- lower_link: int32 [2048, 4], P(('gx', 'gy')), may hold values from 0 to 2048, as said below
- occupation: int32 [2048, 4], P(('gx', 'gy')), may hold values from 0 to 3
Outputs:
- advanced: float32 [2048, 2, 128, 128], P(('gx', 'gy'))
The draws below stay inside these ranges and needn't reach their ends.
Inputs may be any that keep to these rules, and one draw needn't show every extreme that they name: For every bath b, upper_link[g,b] = h with h < 2048 exactly when lower_link[h,b] = g, and then occupation[h,b] = occupation[g,b] + 1; the value 2048 means no link. Matrix g is held by device g // 16, devices numbered in the order gx+gy. lower_link[g,b] < 2048 exactly when occupation[g,b] > 0. Links of the first two baths join two matrices of one device. Links of the third bath join matrices of two devices with the same gx index, and at most one matrix of a device is linked to matrices of any one other device; this bound is reached. Links of the fourth bath join matrices of two devices with the same gy index, and at most 2 matrices of a device are linked to matrices of any one other device; this bound is reached. hamiltonian[0] is symmetric and hamiltonian[1] antisymmetric. Each couplings[b] is symmetric.
All inputs are finite; a program needn't handle non-finite values.
Results may differ from the reference program's by a relative error of at most 0.0001.
Values sent between devices are 32-bit elements; how exact they have to be, the bound alone decides.
No kernel may reach another device: no remote copies, remote signals or barrier semaphores. Data moves between devices by JAX's collectives and lax.ppermute only.
A program may use at most 192 MiB of HBM per device.

```python
import math
import jax
import jax.numpy as jnp
from jax import lax

N = 128
BATHS = 4
CHAIN = 4
XCAP = 2
ADO_DEV = 16
GX_DEVS = 4
GY_DEVS = 32
NADO = 2048


def permute_slots(one_key):
    return jax.random.permutation(one_key, ADO_DEV).astype(jnp.int32)


def permute_rows(one_key):
    return jax.random.permutation(one_key, GY_DEVS).astype(jnp.int32)


def permute_columns(one_key):
    return jax.random.permutation(one_key, GX_DEVS).astype(jnp.int32)


def build_links(base_key):
    devices = GX_DEVS * GY_DEVS
    per_device = ADO_DEV
    missing = NADO
    device_ids = jnp.arange(devices, dtype=jnp.int32)
    upper_table = jnp.full((devices, per_device, BATHS), missing, jnp.int32)
    lower_table = jnp.full((devices, per_device, BATHS), missing, jnp.int32)
    level_table = jnp.zeros((devices, per_device, BATHS), jnp.int32)
    device_rows = jnp.broadcast_to(device_ids[:, None], (devices, per_device))
    chain_place = jnp.broadcast_to(jnp.arange(per_device, dtype=jnp.int32) % CHAIN, (devices, per_device))
    offsets = device_rows * per_device
    for bath_index in range(2):
        shuffle_keys = jax.random.split(jax.random.fold_in(base_key, 11 + bath_index), devices)
        shuffled = jax.vmap(permute_slots)(shuffle_keys)
        following = jnp.roll(shuffled, -1, axis=1)
        preceding = jnp.roll(shuffled, 1, axis=1)
        upper_table = upper_table.at[device_rows, shuffled, bath_index].set(jnp.where(chain_place < CHAIN - 1, offsets + following, missing))
        lower_table = lower_table.at[device_rows, shuffled, bath_index].set(jnp.where(chain_place > 0, offsets + preceding, missing))
        level_table = level_table.at[device_rows, shuffled, bath_index].set(chain_place)
    rounds = min(ADO_DEV // 2, (GY_DEVS - 1) // 2)
    row_labels = jax.vmap(permute_rows)(jax.random.split(jax.random.fold_in(base_key, 21), GX_DEVS))
    row_slots = jax.vmap(permute_slots)(jax.random.split(jax.random.fold_in(base_key, 22), devices))
    present = jax.random.randint(jax.random.fold_in(base_key, 23), (GX_DEVS, GY_DEVS, rounds), 0, 8) > 0
    present = present.at[:, :, 0].set(True)
    grid_shape = (GX_DEVS, GY_DEVS, rounds)
    row_ids = jnp.broadcast_to(jnp.arange(GX_DEVS, dtype=jnp.int32)[:, None, None], grid_shape)
    label_ids = jnp.broadcast_to(jnp.arange(GY_DEVS, dtype=jnp.int32)[None, :, None], grid_shape)
    round_ids = jnp.broadcast_to(jnp.arange(1, rounds + 1, dtype=jnp.int32)[None, None, :], grid_shape)
    lower_device = row_ids * GY_DEVS + row_labels[row_ids, label_ids]
    upper_device = row_ids * GY_DEVS + row_labels[row_ids, (label_ids + round_ids) % GY_DEVS]
    lower_slot = row_slots[lower_device, round_ids - 1]
    upper_slot = row_slots[upper_device, rounds + round_ids - 1]
    upper_table = upper_table.at[lower_device, lower_slot, 2].set(jnp.where(present, upper_device * per_device + upper_slot, missing))
    lower_table = lower_table.at[upper_device, upper_slot, 2].set(jnp.where(present, lower_device * per_device + lower_slot, missing))
    level_table = level_table.at[upper_device, upper_slot, 2].set(jnp.where(present, 1, 0))
    column_labels = jax.vmap(permute_columns)(jax.random.split(jax.random.fold_in(base_key, 31), GY_DEVS))
    column_slots = jax.vmap(permute_slots)(jax.random.split(jax.random.fold_in(base_key, 32), devices))
    pair_shape = (GY_DEVS, GX_DEVS, XCAP)
    column_ids = jnp.broadcast_to(jnp.arange(GY_DEVS, dtype=jnp.int32)[:, None, None], pair_shape)
    position_ids = jnp.broadcast_to(jnp.arange(GX_DEVS, dtype=jnp.int32)[None, :, None], pair_shape)
    pair_ids = jnp.broadcast_to(jnp.arange(XCAP, dtype=jnp.int32)[None, None, :], pair_shape)
    lower_device = column_labels[column_ids, position_ids] * GY_DEVS + column_ids
    upper_device = column_labels[column_ids, (position_ids + 1) % GX_DEVS] * GY_DEVS + column_ids
    lower_slot = column_slots[lower_device, pair_ids]
    upper_slot = column_slots[upper_device, XCAP + pair_ids]
    upper_table = upper_table.at[lower_device, lower_slot, 3].set(upper_device * per_device + upper_slot)
    lower_table = lower_table.at[upper_device, upper_slot, 3].set(lower_device * per_device + lower_slot)
    level_table = level_table.at[upper_device, upper_slot, 3].set(jnp.ones(pair_shape, jnp.int32))
    return (upper_table.reshape(NADO, BATHS), lower_table.reshape(NADO, BATHS), level_table.reshape(NADO, BATHS))


def draw_upper_link(key, part):
    return build_links(jax.random.fold_in(key, 5))[0]


def draw_lower_link(key, part):
    return build_links(jax.random.fold_in(key, 5))[1]


def draw_occupation(key, part):
    return build_links(jax.random.fold_in(key, 5))[2]


def draw_hamiltonian(key, part):
    noise_key, energy_key = jax.random.split(jax.random.fold_in(key, 41))
    noise_draw = jnp.clip(jax.random.normal(noise_key, (2, N, N), jnp.float32), -4.0, 4.0)
    energies = jax.random.uniform(energy_key, (N,), jnp.float32, -1.0, 1.0)
    scale_factor = 1.0 / jnp.sqrt(2.0 * N)
    real_part = (noise_draw[0] + noise_draw[0].T) * scale_factor + jnp.diag(energies)
    imag_part = (noise_draw[1] - noise_draw[1].T) * scale_factor
    return jnp.stack([real_part, imag_part]).astype(jnp.float32)


def draw_couplings(key, part):
    noise_key = jax.random.fold_in(key, 43)
    noise_draw = jnp.clip(jax.random.normal(noise_key, (BATHS, N, N), jnp.float32), -4.0, 4.0)
    return ((noise_draw + jnp.swapaxes(noise_draw, 1, 2)) / jnp.sqrt(2.0 * N)).astype(jnp.float32)


def block_levels(rng, dims, cuts, least, high):
    def one(position, blocks):
        steps = jax.random.uniform(jax.random.fold_in(jax.random.fold_in(rng, 6), position), (blocks,), jnp.float32, least / len(cuts), high / len(cuts))
        return jnp.repeat(jnp.exp(steps), dims[position] // blocks).reshape((-1,) + (1,) * (len(dims) - position - 1))

    factor_of = one(*cuts[0])
    for cut in cuts[1:]:
        factor_of = factor_of * one(*cut)
    return factor_of


def noise(own_key, dims, spread, reach, cuts=(), held_as=jnp.bfloat16):
    array = spread * jax.random.normal(own_key, dims, jnp.float32)
    if cuts:
        array = array * block_levels(own_key, dims, cuts, -0.22, 0.18)
    return jnp.clip(array, -reach, reach).astype(held_as)


def setup_inputs(seed: int = 0) -> dict:
    splits = jax.random.split(jax.random.key(seed), 9)
    return {
        "densities": noise(splits[0], (NADO, 2, N, N), 1.0, 6.0, ((0, 128),), jnp.float32),
        "hamiltonian": draw_hamiltonian(jax.random.fold_in(splits[8], 71), 0),
        "couplings": draw_couplings(jax.random.fold_in(splits[8], 71), 0),
        "decay_rates": jnp.clip(jnp.exp(jax.random.uniform(splits[3], (BATHS,), jnp.float32, math.log(0.5), math.log(2.0))), 0.5, 2.0),
        "correlation": jnp.clip(jax.random.uniform(splits[4], (2, BATHS), jnp.float32, 0.25, 1.5), 0.25, 1.5),
        "upper_link": draw_upper_link(jax.random.fold_in(splits[8], 71), 0),
        "lower_link": draw_lower_link(jax.random.fold_in(splits[8], 71), 0),
        "occupation": draw_occupation(jax.random.fold_in(splits[8], 71), 0),
    }


step_size = 0.1
highest = lax.Precision.HIGHEST


def left_apply(matrix, operand):
    return jnp.einsum("ij,...jk->...ik", matrix, operand, precision=highest)


def right_apply(operand, matrix):
    return jnp.einsum("...ij,jk->...ik", operand, matrix, precision=highest)


def derivative(section_input, hamiltonian, couplings, decay_rates, correlation, upper_link, lower_link, occupation):
    matrix_order = section_input.shape[-1]
    pooled = jnp.concatenate([section_input, jnp.zeros((1, 2, matrix_order, matrix_order), jnp.float32)], axis=0)
    damping = jnp.sum(occupation.astype(jnp.float32) * decay_rates[None, :], axis=1)[:, None, None]
    left_real = left_apply(hamiltonian[0], section_input)
    left_imag = left_apply(hamiltonian[1], section_input)
    right_real = right_apply(section_input, hamiltonian[0])
    right_imag = right_apply(section_input, hamiltonian[1])
    commutator_real = (left_real[:, 0] - left_imag[:, 1]) - (right_real[:, 0] - right_imag[:, 1])
    commutator_imag = (left_real[:, 1] + left_imag[:, 0]) - (right_imag[:, 0] + right_real[:, 1])
    mixed = jnp.zeros_like(section_input)
    for bath_index in range(couplings.shape[0]):
        upper_part = pooled[upper_link[:, bath_index]]
        lower_part = pooled[lower_link[:, bath_index]]
        level_weight = occupation[:, bath_index].astype(jnp.float32)[:, None, None]
        real_weight = correlation[0, bath_index] * level_weight
        imag_weight = correlation[1, bath_index] * level_weight
        forward = jnp.stack([
            upper_part[:, 0] + real_weight * lower_part[:, 0] - imag_weight * lower_part[:, 1],
            upper_part[:, 1] + real_weight * lower_part[:, 1] + imag_weight * lower_part[:, 0]], axis=1)
        backward = jnp.stack([
            upper_part[:, 0] + real_weight * lower_part[:, 0] + imag_weight * lower_part[:, 1],
            upper_part[:, 1] + real_weight * lower_part[:, 1] - imag_weight * lower_part[:, 0]], axis=1)
        mixed = mixed + left_apply(couplings[bath_index], forward) - right_apply(backward, couplings[bath_index])
    out_real = commutator_imag + mixed[:, 1] - damping * section_input[:, 0]
    out_imag = -commutator_real - mixed[:, 0] - damping * section_input[:, 1]
    return jnp.stack([out_real, out_imag], axis=1)


def reference(densities, hamiltonian, couplings, decay_rates, correlation, upper_link, lower_link, occupation):
    def field(section_input):
        return derivative(section_input, hamiltonian, couplings, decay_rates, correlation, upper_link, lower_link, occupation)

    slope_one = field(densities)
    slope_two = field(densities + (0.5 * step_size) * slope_one)
    slope_three = field(densities + (0.5 * step_size) * slope_two)
    slope_four = field(densities + step_size * slope_three)
    return densities + (step_size / 6.0) * (slope_one + 2.0 * slope_two + 2.0 * slope_three + slope_four)
```

```python
import functools

import jax
import jax.numpy as jnp
from jax import lax
from jax.experimental import pallas as pl
from jax.experimental.pallas import tpu as pltpu
from jax.sharding import PartitionSpec as P

XCAP = 2
step_size = 0.1
f32, bf16 = jnp.float32, jnp.bfloat16
HBM = pl.BlockSpec(memory_space=pltpu.HBM)
SMEM = pl.BlockSpec(memory_space=pltpu.SMEM)
VMEM = pl.BlockSpec(memory_space=pltpu.VMEM)


def split(value):
    high = value.astype(bf16)
    return high, (value - high.astype(f32)).astype(bf16)


def prepare_kernel(h_ref, v_ref, left_ref, right_ref, row_left_ref, row_right_ref):
    n = h_ref.shape[-1]

    def put(matrix, left, right, place):
        high, low = split(matrix)
        start = place * 2 * n
        for half in range(2):
            cols = slice(start + half * n, start + (half + 1) * n)
            left[0:n, cols] = high
            left[n : 2 * n, cols] = low
            right[cols, 0:n] = high
            right[cols, n : 2 * n] = low

    terms = [h_ref[1], h_ref[0], v_ref[0], v_ref[1], v_ref[3]]
    for place, matrix in enumerate(terms):
        put(matrix, left_ref, right_ref, place)
    put(v_ref[2], row_left_ref, row_right_ref, 0)


def sandwich(terms, left, right):
    n = terms[0][0][0].shape[-1]
    columns, rows = [], []
    for (la, lb), (ra, rb) in terms:
        columns += [jnp.concatenate(pair, axis=1) for pair in zip(split(la), split(lb))]
        rows += [jnp.concatenate(pair, axis=0) for pair in zip(split(ra), split(rb))]
    stacked = jnp.concatenate(columns, axis=0)
    beside = jnp.concatenate(rows, axis=1)
    ahead = jnp.dot(left, stacked, preferred_element_type=f32)
    behind = jnp.dot(beside, right, preferred_element_type=f32)
    ahead = ahead[0:n] + ahead[n:]
    behind = behind[:, 0:n] + behind[:, n:]
    return ahead[:, 0:n] - behind[0:n], ahead[:, n:] - behind[n:]


def bath_term(ur, ui, lr, li, wr, wi):
    arr, ari, air, aii = wr * lr, wi * lr, wr * li, wi * li
    real, imag = ur + arr, ui + air
    return ((imag + ari, aii - real), (imag - ari, -real - aii))


def local_kernel(tab, wts, z_ref, c1, c2, c3, left, right, *rest, with_sum, last_scale):
    if with_sum:
        acc_ref, *rest = rest
    if last_scale is None and with_sum:
        out_ref, sum_ref, cbuf, sems = rest
    else:
        out_ref, cbuf, sems = rest
    g = pl.program_id(0)

    @pl.when(g == 0)
    def _():
        copies = [
            pltpu.make_async_copy(c, cbuf.at[pl.ds(2 * k, 2)], sems.at[k])
            for k, c in enumerate((c1, c2, c3))
        ]
        for copy in copies:
            copy.start()
        for copy in copies:
            copy.wait()

    yr, yi = z_ref[g, 0], z_ref[g, 1]
    terms = [((yr, yi), (yr, yi)), ((yi, -yr), (yi, -yr))]
    for k, (ref, bath) in enumerate(((z_ref, 0), (z_ref, 1), (cbuf, 3))):
        up, low = tab[g * 8 + 2 + 2 * k], tab[g * 8 + 3 + 2 * k]
        u, l = jnp.maximum(up, 0), jnp.maximum(low, 0)
        ur, ui = (jnp.where(up >= 0, ref[u, part], 0.0) for part in range(2))
        lr, li = (jnp.where(low >= 0, ref[l, part], 0.0) for part in range(2))
        terms.append(bath_term(ur, ui, lr, li, wts[g * 9 + 2 * bath], wts[g * 9 + 2 * bath + 1]))
    out_r, out_i = sandwich(terms, left[...], right[...])
    damp = wts[g * 9 + 8]
    out_r, out_i = out_r - damp * yr, out_i - damp * yi
    if with_sum:
        sum_r, sum_i = acc_ref[0, 0] + yr, acc_ref[0, 1] + yi
    if last_scale is not None:
        out_r, out_i = sum_r + last_scale * out_r, sum_i + last_scale * out_i
    out_ref[0, 0], out_ref[0, 1] = out_r, out_i
    if last_scale is None and with_sum:
        sum_ref[0, 0], sum_ref[0, 1] = sum_r, sum_i


def local_part(tab, wts, z, cols, left, right, acc, last_scale):
    count, _, n, _ = z.shape
    block = pl.BlockSpec((1, 2, n, n), lambda g: (g, 0, 0, 0))
    whole = lambda a: pl.BlockSpec(a.shape, lambda g: (0,) * a.ndim)
    with_sum = acc is not None
    outs = 2 if with_sum and last_scale is None else 1
    shape = pltpu.HBM(z.shape, f32)
    return pl.pallas_call(
        functools.partial(local_kernel, with_sum=with_sum, last_scale=last_scale),
        grid=(count,),
        out_shape=[shape] * outs,
        in_specs=[SMEM, SMEM, whole(z), HBM, HBM, HBM, whole(left), whole(right)]
        + [block] * with_sum,
        out_specs=[block] * outs,
        scratch_shapes=[
            pltpu.VMEM((6, 2, n, n), f32),
            pltpu.SemaphoreType.DMA((3,)),
        ],
        compiler_params=pltpu.CompilerParams(vmem_limit_bytes=16 << 20),
        cost_estimate=pl.CostEstimate(
            flops=count * 20 * 2 * (2 * n) * (2 * n) * n * 4, bytes_accessed=8 << 20, transcendentals=0
        ),
        name="local_part",
    )(tab, wts, z, *cols, left, right, *([acc] if with_sum else []))


def send_rows(tab, g, source, row_out, sem_u, sem_l, go):
    for k, sem in ((0, sem_u), (1, sem_l)):
        slot = tab[g * 8 + k]

        @pl.when(slot >= 0)
        def _():
            copy = pltpu.make_async_copy(source.at[g], row_out.at[jnp.maximum(slot, 0)], sem.at[g])
            copy.start() if go else copy.wait()


def send_columns(ctab, source, outs, sem, go):
    for k in range(6):
        g = ctab[k]

        @pl.when(g >= 0)
        def _():
            copy = pltpu.make_async_copy(
                source.at[jnp.maximum(g, 0)], outs[k // 2].at[k % 2], sem.at[k]
            )
            copy.start() if go else copy.wait()


def pack_rows_kernel(tab, z_ref, row_out, buf, sem_in, sem_u, sem_l):
    count = z_ref.shape[0]
    load = lambda g: pltpu.make_async_copy(z_ref.at[g], buf.at[g], sem_in.at[g])

    @pl.loop(0, count)
    def _(g):
        load(g).start()

    @pl.loop(0, count)
    def _(g):
        load(g).wait()
        send_rows(tab, g, buf, row_out, sem_u, sem_l, True)

    @pl.loop(0, count)
    def _(g):
        send_rows(tab, g, buf, row_out, sem_u, sem_l, False)


def pack_columns_kernel(ctab, z_ref, o1, o2, o3, sem):
    send_columns(ctab, z_ref, (o1, o2, o3), sem, True)
    send_columns(ctab, z_ref, (o1, o2, o3), sem, False)


def row_kernel(tab, ctab, wts, recv, part, left, right, *rest, scale, last):
    count, _, n, _ = part.shape
    if last:
        z_out, ubuf, lbuf, gbuf, zbuf, sem_u, sem_l, sem_g, sem_z = rest
    else:
        (z_out, row_out, o1, o2, o3, ubuf, lbuf, gbuf, zbuf) = rest[:9]
        (sem_u, sem_l, sem_g, sem_z, sem_ru, sem_rl, sem_c) = rest[9:]

    def fetch(g, go):
        for k, buf, sem in ((0, ubuf, sem_u), (1, lbuf, sem_l)):
            slot = tab[g * 8 + k]

            @pl.when(slot >= 0)
            def _():
                copy = pltpu.make_async_copy(recv.at[jnp.maximum(slot, 0)], buf.at[g], sem.at[g])
                copy.start() if go else copy.wait()

        copy = pltpu.make_async_copy(part.at[g], gbuf.at[g], sem_g.at[g])
        copy.start() if go else copy.wait()

    def keep(g):
        return pltpu.make_async_copy(zbuf.at[g], z_out.at[g], sem_z.at[g])

    @pl.loop(0, count)
    def _(g):
        fetch(g, True)

    def one(g):
        up, low = tab[g * 8], tab[g * 8 + 1]
        ur, ui = (jnp.where(up >= 0, ubuf[g, p], 0.0) for p in range(2))
        lr, li = (jnp.where(low >= 0, lbuf[g, p], 0.0) for p in range(2))
        term = bath_term(ur, ui, lr, li, wts[g * 9 + 4], wts[g * 9 + 5])
        out_r, out_i = sandwich([term], left[...], right[...])
        if last:
            zbuf[g, 0] = gbuf[g, 0] + scale * out_r
            zbuf[g, 1] = gbuf[g, 1] + scale * out_i
        else:
            zbuf[g, 0] = scale * (gbuf[g, 0] + out_r)
            zbuf[g, 1] = scale * (gbuf[g, 1] + out_i)

    width = 4

    @pl.loop(0, count // width)
    def _(step):
        for k in range(width):
            fetch(step * width + k, False)
        for k in range(width):
            one(step * width + k)
        for k in range(width):
            g = step * width + k
            keep(g).start()
            if not last:
                send_rows(tab, g, zbuf, row_out, sem_ru, sem_rl, True)

    if not last:
        send_columns(ctab, zbuf, (o1, o2, o3), sem_c, True)

    @pl.loop(0, count)
    def _(g):
        keep(g).wait()
        if not last:
            send_rows(tab, g, zbuf, row_out, sem_ru, sem_rl, False)

    if not last:
        send_columns(ctab, zbuf, (o1, o2, o3), sem_c, False)


def row_part(tab, ctab, wts, recv, part, left, right, scale, last):
    count, _, n, _ = part.shape
    shape = lambda rows: pltpu.HBM((rows, 2, n, n), f32)
    outs = [jax.ShapeDtypeStruct(part.shape, f32) if last else shape(count)]
    if not last:
        outs += [shape(recv.shape[0])] + [shape(XCAP)] * 3
    sems = [pltpu.SemaphoreType.DMA((count,))] * (4 if last else 6)
    if not last:
        sems = sems + [pltpu.SemaphoreType.DMA((6,))]
    return pl.pallas_call(
        functools.partial(row_kernel, scale=scale, last=last),
        out_shape=outs,
        in_specs=[SMEM, SMEM, SMEM, HBM, HBM, VMEM, VMEM],
        out_specs=[HBM] * len(outs),
        scratch_shapes=[pltpu.VMEM((count, 2, n, n), f32)] * 4 + sems,
        compiler_params=pltpu.CompilerParams(vmem_limit_bytes=16 << 20),
        cost_estimate=pl.CostEstimate(
            flops=count * 16 * 2 * n * n * n, bytes_accessed=10 << 20, transcendentals=0
        ),
        name="row_part",
    )(tab, ctab, wts, *(pltpu.with_memory_space_constraint(a, pltpu.HBM) for a in (recv, part)), left, right)


def local(
    densities, hamiltonian, couplings, decay_rates, correlation, upper_link, lower_link, occupation
):
    count, _, n, _ = densities.shape
    along_y, along_x = lax.axis_size("gy"), lax.axis_size("gx")
    index_x, index_y = lax.axis_index("gx"), lax.axis_index("gy")
    own = index_x * along_y + index_y
    missing = count * along_y * along_x

    links = jnp.stack([upper_link, lower_link], axis=2)
    live = links < missing
    near = jnp.where(live[:, 0:2], links[:, 0:2] - own * count, -1).reshape(count, 4)
    rows = jnp.where(live[:, 2], (links[:, 2] // count) % along_y, -1)

    targets, usable = links[:, 3].reshape(-1), live[:, 3].reshape(-1)
    sources = jnp.repeat(jnp.arange(count, dtype=jnp.int32), 2)
    relative = (targets // count // along_y - index_x) % along_x
    same = usable[:, None] & usable[None, :] & (relative[:, None] == relative[None, :])
    start = (relative - 1) * XCAP
    recv_slot = start + jnp.any(same & (targets[None, :] < targets[:, None]), axis=1)
    send_slot = start + jnp.any(same & (sources[None, :] < sources[:, None]), axis=1)
    recv_slot = jnp.where(usable, recv_slot, -1).reshape(count, 2)
    hit = (send_slot[None, :] == jnp.arange(6, dtype=jnp.int32)[:, None]) & usable[None, :]
    ctab = jnp.max(jnp.where(hit, sources[None, :], -1), axis=1)
    tab = jnp.concatenate([rows, near, recv_slot], axis=1).reshape(-1).astype(jnp.int32)

    level = occupation.astype(f32)
    damping = jnp.sum(level * decay_rates[None, :], axis=1, keepdims=True)
    pairs = (level[:, :, None] * correlation.T[None, :, :]).reshape(count, 8)
    wts = jnp.concatenate([pairs, damping], axis=1).reshape(-1)

    mats = lambda rows, cols: jax.ShapeDtypeStruct((rows, cols), bf16)
    left, right, row_left, row_right = pl.pallas_call(
        prepare_kernel,
        out_shape=[mats(2 * n, 10 * n), mats(10 * n, 2 * n), mats(2 * n, 2 * n), mats(2 * n, 2 * n)],
        in_specs=[VMEM, VMEM],
        out_specs=[VMEM] * 4,
        name="prepare",
    )(hamiltonian, couplings)

    row_send = pl.pallas_call(
        pack_rows_kernel,
        out_shape=pltpu.HBM((along_y, 2, n, n), f32),
        in_specs=[SMEM, HBM],
        out_specs=HBM,
        scratch_shapes=[pltpu.VMEM((count, 2, n, n), f32)]
        + [pltpu.SemaphoreType.DMA((count,))] * 3,
        name="pack_rows",
    )(tab, densities)
    col_send = pl.pallas_call(
        pack_columns_kernel,
        out_shape=[pltpu.HBM((XCAP, 2, n, n), f32)] * 3,
        in_specs=[SMEM, VMEM],
        out_specs=[HBM] * 3,
        scratch_shapes=[pltpu.SemaphoreType.DMA((6,))],
        name="pack_columns",
    )(ctab, densities)

    z, acc = densities, None
    for stage in range(1, 5):
        recv = lax.all_to_all(row_send, "gy", split_axis=0, concat_axis=0, tiled=True)
        arrived = [
            lax.ppermute(col_send[s - 1], "gx", [(x, (x + s) % along_x) for x in range(along_x)])
            for s in range(1, along_x)
        ]
        cols = arrived[::-1]
        scale, last = step_size / stage, stage == 4
        part = local_part(
            tab, wts, z, cols, left, right, acc, scale if last else None
        )
        if stage == 1:
            acc = densities
        elif not last:
            acc = part[1]
        outs = row_part(tab, ctab, wts, recv, part[0], row_left, row_right, scale, last)
        if last:
            return outs[0]
        z, row_send, *col_send = outs


def solution(mesh):
    return jax.shard_map(
        local,
        mesh=mesh,
        in_specs=(
            P(("gx", "gy"), None, None, None),
            P(),
            P(),
            P(),
            P(),
            P(("gx", "gy"), None),
            P(("gx", "gy"), None),
            P(("gx", "gy"), None),
        ),
        out_specs=P(("gx", "gy"), None, None, None),
        check_vma=False,
    )
```

```python
import functools

import jax
import jax.numpy as jnp
from jax import lax
from jax.experimental import pallas as pl
from jax.experimental.pallas import tpu as pltpu
from jax.sharding import PartitionSpec as P

XCAP = 2
step_size = 0.1
f32, bf16 = jnp.float32, jnp.bfloat16
LIMIT = 24 << 20
WIDTH = 4
HBM = pl.BlockSpec(memory_space=pltpu.HBM)
SMEM = pl.BlockSpec(memory_space=pltpu.SMEM)
VMEM = pl.BlockSpec(memory_space=pltpu.VMEM)


def split(value):
    high = value.astype(bf16)
    return high, (value - high.astype(f32)).astype(bf16)


def prepare_kernel(h_ref, v_ref, left_ref, right_ref, row_left_ref, row_right_ref):
    n = h_ref.shape[-1]

    def put(matrix, left, right, place):
        high, low = split(matrix)
        start = place * 2 * n
        for half in range(2):
            cols = slice(start + half * n, start + (half + 1) * n)
            left[0:n, cols] = high
            left[n : 2 * n, cols] = low
            right[cols, 0:n] = high
            right[cols, n : 2 * n] = low

    terms = [h_ref[1], h_ref[0], v_ref[0], v_ref[1], v_ref[3]]
    for place, matrix in enumerate(terms):
        put(matrix, left_ref, right_ref, place)
    put(v_ref[2], row_left_ref, row_right_ref, 0)


def sandwich(terms, left, right):
    n = terms[0][0][0].shape[-1]
    columns, rows = [], []
    for (la, lb), (ra, rb) in terms:
        columns += [jnp.concatenate(pair, axis=1) for pair in zip(split(la), split(lb))]
        rows += [jnp.concatenate(pair, axis=0) for pair in zip(split(ra), split(rb))]
    stacked = jnp.concatenate(columns, axis=0)
    beside = jnp.concatenate(rows, axis=1)
    ahead = jnp.dot(left, stacked, preferred_element_type=f32)
    behind = jnp.dot(beside, right, preferred_element_type=f32)
    ahead = ahead[0:n] + ahead[n:]
    behind = behind[:, 0:n] + behind[:, n:]
    return ahead[:, 0:n] - behind[0:n], ahead[:, n:] - behind[n:]


def bath_term(ur, ui, lr, li, wr, wi):
    arr, ari, air, aii = wr * lr, wi * lr, wr * li, wi * li
    real, imag = ur + arr, ui + air
    return ((imag + ari, aii - real), (imag - ari, -real - aii))


def first_slot(tab, g):
    up, low = tab[g * 8], tab[g * 8 + 1]
    return jnp.where(up >= 0, up, low)


def when_copy(live, source, target, sem, go):
    @pl.when(live)
    def _():
        copy = pltpu.make_async_copy(source, target, sem)
        copy.start() if go else copy.wait()


def load_state(tab, g, state, buf, sem, go):
    if len(state) == 1:
        when_copy(g >= 0, state[0].at[jnp.maximum(g, 0)], buf, sem, go)
        return
    slot = first_slot(tab, jnp.maximum(g, 0))
    when_copy((g >= 0) & (slot >= 0), state[1].at[jnp.maximum(slot, 0)], buf, sem, go)
    when_copy((g >= 0) & (slot < 0), state[0].at[jnp.maximum(g, 0)], buf, sem, go)


def local_kernel(tab, wts, c1, c2, c3, left, right, *rest, states, with_sum, last_scale):
    state, rest = rest[:states], rest[states:]
    count = state[0].shape[0]
    if with_sum:
        acc_ref, *rest = rest
    keep_sum = with_sum and last_scale is None
    if keep_sum:
        out_ref, sum_ref, z_ref, cbuf, sem_z, sems = rest
    else:
        out_ref, z_ref, cbuf, sem_z, sems = rest

    @pl.loop(0, count)
    def _(g):
        load_state(tab, g, state, z_ref.at[g], sem_z.at[g], True)

    copies = [
        pltpu.make_async_copy(c, cbuf.at[pl.ds(XCAP * k, XCAP)], sems.at[k])
        for k, c in enumerate((c1, c2, c3))
    ]
    for copy in copies:
        copy.start()
    for copy in copies:
        copy.wait()

    @pl.loop(0, count)
    def _(g):
        load_state(tab, g, state, z_ref.at[g], sem_z.at[g], False)

    def one(g):
        yr, yi = z_ref[g, 0], z_ref[g, 1]
        terms = [((yr, yi), (yr, yi)), ((yi, -yr), (yi, -yr))]
        for k, (ref, bath) in enumerate(((z_ref, 0), (z_ref, 1), (cbuf, 3))):
            up, low = tab[g * 8 + 2 + 2 * k], tab[g * 8 + 3 + 2 * k]
            u, l = jnp.maximum(up, 0), jnp.maximum(low, 0)
            ur, ui = (jnp.where(up >= 0, ref[u, part], 0.0) for part in range(2))
            lr, li = (jnp.where(low >= 0, ref[l, part], 0.0) for part in range(2))
            wr, wi = wts[g * 9 + 2 * bath], wts[g * 9 + 2 * bath + 1]
            terms.append(bath_term(ur, ui, lr, li, wr, wi))
        out_r, out_i = sandwich(terms, left[...], right[...])
        damp = wts[g * 9 + 8]
        out_r, out_i = out_r - damp * yr, out_i - damp * yi
        if with_sum:
            sum_r, sum_i = acc_ref[g, 0] + yr, acc_ref[g, 1] + yi
        if last_scale is not None:
            out_r, out_i = sum_r + last_scale * out_r, sum_i + last_scale * out_i
        out_ref[g, 0], out_ref[g, 1] = out_r, out_i
        if keep_sum:
            sum_ref[g, 0], sum_ref[g, 1] = sum_r, sum_i

    width = 2

    @pl.loop(0, count // width)
    def _(step):
        for k in range(width):
            one(step * width + k)


def in_hbm(*arrays):
    return [pltpu.with_memory_space_constraint(a, pltpu.HBM) for a in arrays]


def local_part(tab, wts, state, cols, left, right, acc, last_scale):
    count, _, n, _ = state[0].shape
    with_sum = acc is not None
    outs = 2 if with_sum and last_scale is None else 1
    return pl.pallas_call(
        functools.partial(
            local_kernel, states=len(state), with_sum=with_sum, last_scale=last_scale
        ),
        out_shape=[jax.ShapeDtypeStruct(state[0].shape, f32)] * outs,
        in_specs=[SMEM, SMEM, HBM, HBM, HBM, VMEM, VMEM]
        + [HBM] * len(state)
        + [VMEM] * with_sum,
        out_specs=[VMEM] * outs,
        scratch_shapes=[
            pltpu.VMEM((count, 2, n, n), f32),
            pltpu.VMEM((3 * XCAP, 2, n, n), f32),
            pltpu.SemaphoreType.DMA((count,)),
            pltpu.SemaphoreType.DMA((3,)),
        ],
        compiler_params=pltpu.CompilerParams(vmem_limit_bytes=LIMIT),
        cost_estimate=pl.CostEstimate(
            flops=count * 160 * n * n * n, bytes_accessed=8 << 20, transcendentals=0
        ),
        name="local_part",
    )(tab, wts, *cols, left, right, *in_hbm(*state), *([acc] if with_sum else []))


def pack_columns_kernel(tab, ctab, *rest, states):
    state, (o1, o2, o3, buf, sem) = rest[:states], rest[states:]
    outs = (o1, o2, o3)
    slots = len(outs) * XCAP
    for go in (True, False):
        for k in range(slots):
            load_state(tab, ctab[k], state, buf.at[k], sem.at[k], go)
    for go in (True, False):
        for k in range(slots):
            when_copy(ctab[k] >= 0, buf.at[k], outs[k // XCAP].at[k % XCAP], sem.at[k], go)


def pack_columns(tab, ctab, state):
    count, _, n, _ = state[0].shape
    return pl.pallas_call(
        functools.partial(pack_columns_kernel, states=len(state)),
        out_shape=[pltpu.HBM((XCAP, 2, n, n), f32)] * 3,
        in_specs=[SMEM, SMEM] + [HBM] * len(state),
        out_specs=[HBM] * 3,
        scratch_shapes=[
            pltpu.VMEM((3 * XCAP, 2, n, n), f32),
            pltpu.SemaphoreType.DMA((3 * XCAP,)),
        ],
        cost_estimate=pl.CostEstimate(flops=0, bytes_accessed=1 << 20, transcendentals=0),
        name="pack_columns",
    )(tab, ctab, *in_hbm(*state))


def pack_rows_kernel(up_ref, low_ref, z_ref, row_out, buf, sem_in, sem_u, sem_l, *, missing, bath):
    count, along_y = z_ref.shape[0], row_out.shape[0]
    links = ((up_ref, sem_u), (low_ref, sem_l))

    def load(g, go):
        linked = (up_ref[g, bath] < missing) | (low_ref[g, bath] < missing)
        when_copy(linked, z_ref.at[g], buf.at[g], sem_in.at[g], go)

    def send(g, go):
        for ref, sem in links:
            target = ref[g, bath]
            slot = lax.rem(lax.div(target, count), along_y)
            when_copy(target < missing, buf.at[g], row_out.at[slot], sem.at[g], go)

    @pl.loop(0, count)
    def _(g):
        load(g, True)

    @pl.loop(0, count)
    def _(g):
        load(g, False)
        send(g, True)

    @pl.loop(0, count)
    def _(g):
        send(g, False)


def row_kernel(tab, wts, recv, part, left, right, *rest, scale, last):
    count, _, n, _ = part.shape
    if last:
        z_out, xbuf, ybuf, zbuf, sem_x, sem_y, sem_g, sem_z = rest
    else:
        z_out, row_out, xbuf, ybuf, zbuf, sem_x, sem_y, sem_g, sem_z, sem_u, sem_l = rest

    def both(g):
        return (tab[g * 8] >= 0) & (tab[g * 8 + 1] >= 0)

    def fetch(g, go):
        slot, low = first_slot(tab, g), tab[g * 8 + 1]
        when_copy(slot >= 0, recv.at[jnp.maximum(slot, 0)], xbuf.at[g], sem_x.at[g], go)
        when_copy(both(g), recv.at[jnp.maximum(low, 0)], ybuf.at[g], sem_y.at[g], go)
        if go:

            @pl.when(slot < 0)
            def _():
                xbuf[g] = jnp.zeros_like(xbuf[g])

    def fetch_part(step):
        group = pl.ds(step * WIDTH, WIDTH)
        return pltpu.make_async_copy(part.at[group], zbuf.at[group], sem_g.at[step])

    def send(g, go):
        if last:
            when_copy(g >= 0, zbuf.at[g], z_out.at[g], sem_z.at[g], go)
            return
        for k, sem in ((0, sem_u), (1, sem_l)):
            slot = tab[g * 8 + k]
            when_copy(slot >= 0, zbuf.at[g], row_out.at[jnp.maximum(slot, 0)], sem.at[g], go)
        when_copy(first_slot(tab, g) < 0, zbuf.at[g], z_out.at[g], sem_z.at[g], go)

    @pl.loop(0, count // WIDTH)
    def _(step):
        for k in range(WIDTH):
            fetch(step * WIDTH + k, True)
        fetch_part(step).start()

    def product(buf, group, reals, imags):
        ahead, beside = [], []
        for g in group:
            (hr, tr), (hi, ti) = split(buf[g, 0]), split(buf[g, 1])
            high, tail = jnp.concatenate([hr, hi], 1), jnp.concatenate([tr, ti], 1)
            stacked = jnp.concatenate([high, tail], 0)
            both_rows = jnp.dot(left[...], stacked, preferred_element_type=f32)
            ahead.append(both_rows[0:n] + both_rows[n:])
            beside.append(jnp.concatenate([hr, tr], 1))
            beside.append(jnp.concatenate([hi, ti], 1))
        behind = jnp.dot(jnp.concatenate(beside, 0), right[...], preferred_element_type=f32)
        behind = behind[:, 0:n] + behind[:, n:]
        for k, (real, imag) in enumerate(zip(reals, imags)):
            ar, ai = ahead[k][:, 0:n], ahead[k][:, n:]
            br, bi = (behind[(2 * k + p) * n : (2 * k + p + 1) * n] for p in range(2))
            yield real * (ai - bi) + imag * (ar + br), imag * (ai + bi) - real * (ar - br)

    def weights(g):
        return wts[g * 9 + 4], wts[g * 9 + 5]

    @pl.loop(0, count // WIDTH)
    def _(step):
        group = [step * WIDTH + k for k in range(WIDTH)]
        for g in group:
            fetch(g, False)
        fetch_part(step).wait()
        above = [tab[g * 8] >= 0 for g in group]
        reals = [jnp.where(a, 1.0, weights(g)[0]) for a, g in zip(above, group)]
        imags = [jnp.where(a, 0.0, weights(g)[1]) for a, g in zip(above, group)]
        for g, term in zip(group, product(xbuf, group, reals, imags)):
            for p in range(2):
                if last:
                    zbuf[g, p] = zbuf[g, p] + scale * term[p]
                else:
                    zbuf[g, p] = scale * (zbuf[g, p] + term[p])
        for g in group:

            @pl.when(both(g))
            def _():
                wr, wi = weights(g)
                (term,) = product(ybuf, [g], [wr], [wi])
                for p in range(2):
                    zbuf[g, p] = zbuf[g, p] + scale * term[p]

        for g in group:
            send(g, True)

    @pl.loop(0, count)
    def _(g):
        send(g, False)


def row_part(tab, wts, recv, part, left, right, scale, last):
    count, _, n, _ = part.shape
    outs = [jax.ShapeDtypeStruct(part.shape, f32) if last else pltpu.HBM(part.shape, f32)]
    if not last:
        outs += [pltpu.HBM(recv.shape, f32)]
    return pl.pallas_call(
        functools.partial(row_kernel, scale=scale, last=last),
        out_shape=outs,
        in_specs=[SMEM, SMEM, HBM, HBM, VMEM, VMEM],
        out_specs=[HBM] * len(outs),
        scratch_shapes=[pltpu.VMEM((count, 2, n, n), f32)] * 3
        + [pltpu.SemaphoreType.DMA((count,))] * (4 if last else 6),
        compiler_params=pltpu.CompilerParams(vmem_limit_bytes=LIMIT),
        cost_estimate=pl.CostEstimate(
            flops=count * 32 * n * n * n, bytes_accessed=10 << 20, transcendentals=0
        ),
        name="row_part",
    )(tab, wts, *in_hbm(recv, part), left, right)


def local(
    densities, hamiltonian, couplings, decay_rates, correlation, upper_link, lower_link, occupation
):
    count, _, n, _ = densities.shape
    along_y, along_x = lax.axis_size("gy"), lax.axis_size("gx")
    index_x, index_y = lax.axis_index("gx"), lax.axis_index("gy")
    own = index_x * along_y + index_y
    missing = count * along_y * along_x

    row_send = pl.pallas_call(
        functools.partial(pack_rows_kernel, missing=missing, bath=2),
        out_shape=pltpu.HBM((along_y, 2, n, n), f32),
        in_specs=[SMEM, SMEM, HBM],
        out_specs=HBM,
        scratch_shapes=[pltpu.VMEM((count, 2, n, n), f32)]
        + [pltpu.SemaphoreType.DMA((count,))] * 3,
        name="pack_rows",
    )(upper_link, lower_link, densities)

    links = jnp.stack([upper_link, lower_link], axis=2)
    live = links < missing
    near = jnp.where(live[:, 0:2], links[:, 0:2] - own * count, -1).reshape(count, 4)
    rows = jnp.where(live[:, 2], (links[:, 2] // count) % along_y, -1)

    targets, usable = links[:, 3].reshape(-1), live[:, 3].reshape(-1)
    sources = jnp.repeat(jnp.arange(count, dtype=jnp.int32), 2)
    relative = (targets // count // along_y - index_x) % along_x
    same = usable[:, None] & usable[None, :] & (relative[:, None] == relative[None, :])
    start = (relative - 1) * XCAP
    recv_slot = start + jnp.any(same & (targets[None, :] < targets[:, None]), axis=1)
    send_slot = start + jnp.any(same & (sources[None, :] < sources[:, None]), axis=1)
    recv_slot = jnp.where(usable, recv_slot, -1).reshape(count, 2)
    hit = (send_slot[None, :] == jnp.arange(6, dtype=jnp.int32)[:, None]) & usable[None, :]
    ctab = jnp.max(jnp.where(hit, sources[None, :], -1), axis=1)
    tab = jnp.concatenate([rows, near, recv_slot], axis=1).reshape(-1).astype(jnp.int32)

    level = occupation.astype(f32)
    damping = jnp.sum(level * decay_rates[None, :], axis=1, keepdims=True)
    pairs = (level[:, :, None] * correlation.T[None, :, :]).reshape(count, 8)
    wts = jnp.concatenate([pairs, damping], axis=1).reshape(-1)

    mats = lambda rows, cols: jax.ShapeDtypeStruct((rows, cols), bf16)
    left, right, row_left, row_right = pl.pallas_call(
        prepare_kernel,
        out_shape=[mats(2 * n, 10 * n), mats(10 * n, 2 * n), mats(2 * n, 2 * n), mats(2 * n, 2 * n)],
        in_specs=[VMEM, VMEM],
        out_specs=[VMEM] * 4,
        name="prepare",
    )(hamiltonian, couplings)

    state, acc = [densities], None
    for stage in range(1, 5):
        recv = lax.all_to_all(row_send, "gy", split_axis=0, concat_axis=0, tiled=True)
        col_send = pack_columns(tab, ctab, state)
        arrived = [
            lax.ppermute(col_send[s - 1], "gx", [(x, (x + s) % along_x) for x in range(along_x)])
            for s in range(1, along_x)
        ]
        scale, last = step_size / stage, stage == 4
        part = local_part(
            tab, wts, state, arrived[::-1], left, right, acc, scale if last else None
        )
        if stage == 1:
            acc = densities
        elif not last:
            acc = part[1]
        outs = row_part(tab, wts, recv, part[0], row_left, row_right, scale, last)
        if last:
            return outs[0]
        state, row_send = outs, outs[1]


def solution(mesh):
    return jax.shard_map(
        local,
        mesh=mesh,
        in_specs=(
            P(("gx", "gy"), None, None, None),
            P(),
            P(),
            P(),
            P(),
            P(("gx", "gy"), None),
            P(("gx", "gy"), None),
            P(("gx", "gy"), None),
        ),
        out_specs=P(("gx", "gy"), None, None, None),
        check_vma=False,
    )
```

```python
import functools

import jax
import jax.numpy as jnp
from jax import lax
from jax.experimental import pallas as pl
from jax.experimental.pallas import tpu as pltpu
from jax.sharding import PartitionSpec as P

XCAP = 2
step_size = 0.1
f32, bf16 = jnp.float32, jnp.bfloat16
LIMIT = 24 << 20
WIDTH = 4
SCALARS = 11
HBM = pl.BlockSpec(memory_space=pltpu.HBM)
SMEM = pl.BlockSpec(memory_space=pltpu.SMEM)
VMEM = pl.BlockSpec(memory_space=pltpu.VMEM)


def split(value):
    high = value.astype(bf16)
    return high, (value - high.astype(f32)).astype(bf16)


def prepare_kernel(h_ref, v_ref, left_ref, right_ref, row_left_ref, row_right_ref):
    n = h_ref.shape[-1]

    def put(matrix, left, right, place):
        high, low = split(matrix)
        start = place * 2 * n
        for half in range(2):
            cols = slice(start + half * n, start + (half + 1) * n)
            left[0:n, cols] = high
            left[n : 2 * n, cols] = low
            right[cols, 0:n] = high
            right[cols, n : 2 * n] = low

    terms = [h_ref[1], h_ref[0], v_ref[0], v_ref[1], v_ref[3]]
    for place, matrix in enumerate(terms):
        put(matrix, left_ref, right_ref, place)
    put(v_ref[2], row_left_ref, row_right_ref, 0)


def sandwich(terms, left, right):
    n = terms[0][0][0].shape[-1]
    columns, rows = [], []
    for (la, lb), (ra, rb) in terms:
        columns += [jnp.concatenate(pair, axis=1) for pair in zip(split(la), split(lb))]
        rows += [jnp.concatenate(pair, axis=0) for pair in zip(split(ra), split(rb))]
    stacked = jnp.concatenate(columns, axis=0)
    beside = jnp.concatenate(rows, axis=1)
    ahead = jnp.dot(left, stacked, preferred_element_type=f32)
    behind = jnp.dot(beside, right, preferred_element_type=f32)
    ahead = ahead[0:n] + ahead[n:]
    behind = behind[:, 0:n] + behind[:, n:]
    return ahead[:, 0:n] - behind[0:n], ahead[:, n:] - behind[n:]


def bath_term(ur, ui, lr, li, wr, wi):
    arr, ari, air, aii = wr * lr, wi * lr, wr * li, wi * li
    real, imag = ur + arr, ui + air
    return ((imag + ari, aii - real), (imag - ari, -real - aii))


def first_slot(tab, g):
    up, low = tab[g * 8], tab[g * 8 + 1]
    return jnp.where(up >= 0, up, low)


def when_copy(live, source, target, sem, go):
    @pl.when(live)
    def _():
        copy = pltpu.make_async_copy(source, target, sem)
        copy.start() if go else copy.wait()


def send_slots(tab, g, buf, row_out, sem_u, sem_l, go):
    for k, sem in ((0, sem_u), (1, sem_l)):
        slot = tab[g * 8 + k]
        when_copy(slot >= 0, buf.at[g], row_out.at[jnp.maximum(slot, 0)], sem.at[g], go)


def local_kernel(tab, wts, z_ref, c1, c2, c3, left, right, *rest, with_sum, last_scale):
    count = z_ref.shape[0]
    if with_sum:
        acc_ref, *rest = rest
    last = last_scale is not None
    keep_sum = with_sum and not last
    out_ref, *rest = rest
    if not last:
        row_out, *rest = rest
    if keep_sum:
        sum_ref, *rest = rest
    cbuf, sems, sem_u, sem_l = rest

    copies = [
        pltpu.make_async_copy(c, cbuf.at[pl.ds(XCAP * k, XCAP)], sems.at[k])
        for k, c in enumerate((c1, c2, c3))
    ]
    for copy in copies:
        copy.start()
    for copy in copies:
        copy.wait()

    def one(g):
        yr, yi = z_ref[g, 0], z_ref[g, 1]
        terms = [((yr, yi), (yr, yi)), ((yi, -yr), (yi, -yr))]
        for k, (ref, bath) in enumerate(((z_ref, 0), (z_ref, 1), (cbuf, 3))):
            up, low = tab[g * 8 + 2 + 2 * k], tab[g * 8 + 3 + 2 * k]
            u, l = jnp.maximum(up, 0), jnp.maximum(low, 0)
            ur, ui = (jnp.where(up >= 0, ref[u, part], 0.0) for part in range(2))
            lr, li = (jnp.where(low >= 0, ref[l, part], 0.0) for part in range(2))
            wr, wi = wts[g * SCALARS + 2 * bath], wts[g * SCALARS + 2 * bath + 1]
            terms.append(bath_term(ur, ui, lr, li, wr, wi))
        out_r, out_i = sandwich(terms, left[...], right[...])
        damp = wts[g * SCALARS + 8]
        out_r, out_i = out_r - damp * yr, out_i - damp * yi
        if with_sum:
            sum_r, sum_i = acc_ref[g, 0] + yr, acc_ref[g, 1] + yi
        if last_scale is not None:
            out_r, out_i = sum_r + last_scale * out_r, sum_i + last_scale * out_i
        out_ref[g, 0], out_ref[g, 1] = out_r, out_i
        if keep_sum:
            sum_ref[g, 0], sum_ref[g, 1] = sum_r, sum_i

    width = 2

    @pl.loop(0, count // width)
    def _(step):
        for k in range(width):
            one(step * width + k)
        if not last:
            for k in range(width):
                send_slots(tab, step * width + k, out_ref, row_out, sem_u, sem_l, True)

    if not last:

        @pl.loop(0, count)
        def _(g):
            send_slots(tab, g, out_ref, row_out, sem_u, sem_l, False)


def in_hbm(*arrays):
    return [pltpu.with_memory_space_constraint(a, pltpu.HBM) for a in arrays]


def local_part(tab, wts, z, cols, left, right, acc, slots, last_scale):
    count, _, n, _ = z.shape
    with_sum, last = acc is not None, last_scale is not None
    outs, places = [jax.ShapeDtypeStruct(z.shape, f32)], [VMEM]
    if not last:
        outs, places = outs + [pltpu.HBM((slots, 2, n, n), f32)], places + [HBM]
    if with_sum and not last:
        outs, places = outs + [jax.ShapeDtypeStruct(z.shape, f32)], places + [VMEM]
    return pl.pallas_call(
        functools.partial(local_kernel, with_sum=with_sum, last_scale=last_scale),
        out_shape=outs,
        in_specs=[SMEM, SMEM, VMEM, HBM, HBM, HBM, VMEM, VMEM] + [VMEM] * with_sum,
        out_specs=places,
        scratch_shapes=[
            pltpu.VMEM((3 * XCAP, 2, n, n), f32),
            pltpu.SemaphoreType.DMA((3,)),
            pltpu.SemaphoreType.DMA((count,)),
            pltpu.SemaphoreType.DMA((count,)),
        ],
        compiler_params=pltpu.CompilerParams(vmem_limit_bytes=LIMIT),
        cost_estimate=pl.CostEstimate(
            flops=count * 160 * n * n * n, bytes_accessed=8 << 20, transcendentals=0
        ),
        name="local_part",
    )(tab, wts, z, *cols, left, right, *([acc] if with_sum else []))


def pack_columns_kernel(ctab, z_ref, o1, o2, o3, buf, sem):
    outs = (o1, o2, o3)
    slots = len(outs) * XCAP
    for go in (True, False):
        for k in range(slots):
            g = ctab[k]
            when_copy(g >= 0, z_ref.at[jnp.maximum(g, 0)], buf.at[k], sem.at[k], go)
    for go in (True, False):
        for k in range(slots):
            when_copy(ctab[k] >= 0, buf.at[k], outs[k // XCAP].at[k % XCAP], sem.at[k], go)


def pack_columns(ctab, z):
    count, _, n, _ = z.shape
    return pl.pallas_call(
        pack_columns_kernel,
        out_shape=[pltpu.HBM((XCAP, 2, n, n), f32)] * 3,
        in_specs=[SMEM, HBM],
        out_specs=[HBM] * 3,
        scratch_shapes=[
            pltpu.VMEM((3 * XCAP, 2, n, n), f32),
            pltpu.SemaphoreType.DMA((3 * XCAP,)),
        ],
        cost_estimate=pl.CostEstimate(flops=0, bytes_accessed=1 << 20, transcendentals=0),
        name="pack_columns",
    )(ctab, *in_hbm(z))


def pack_rows_kernel(up_ref, low_ref, z_ref, row_out, buf, sem_in, sem_u, sem_l, *, missing, bath):
    count, along_y = z_ref.shape[0], row_out.shape[0]
    links = ((up_ref, sem_u), (low_ref, sem_l))

    def load(g, go):
        linked = (up_ref[bath, g] < missing) | (low_ref[bath, g] < missing)
        when_copy(linked, z_ref.at[g], buf.at[g], sem_in.at[g], go)

    def send(g, go):
        for ref, sem in links:
            target = ref[bath, g]
            slot = lax.rem(lax.div(target, count), along_y)
            when_copy(target < missing, buf.at[g], row_out.at[slot], sem.at[g], go)

    @pl.loop(0, count)
    def _(g):
        load(g, True)

    @pl.loop(0, count)
    def _(g):
        load(g, False)
        send(g, True)

    @pl.loop(0, count)
    def _(g):
        send(g, False)


def product(left, right, values, reals, imags):
    n = values[0][0].shape[-1]
    ahead, beside = [], []
    for xr, xi in values:
        (hr, tr), (hi, ti) = split(xr), split(xi)
        high, tail = jnp.concatenate([hr, hi], 1), jnp.concatenate([tr, ti], 1)
        rows = jnp.dot(left, jnp.concatenate([high, tail], 0), preferred_element_type=f32)
        ahead.append(rows[0:n] + rows[n:])
        beside.append(jnp.concatenate([hr, tr], 1))
        beside.append(jnp.concatenate([hi, ti], 1))
    behind = jnp.dot(jnp.concatenate(beside, 0), right, preferred_element_type=f32)
    behind = behind[:, 0:n] + behind[:, n:]
    results = []
    for k, (real, imag) in enumerate(zip(reals, imags)):
        ar, ai = ahead[k][:, 0:n], ahead[k][:, n:]
        br, bi = (behind[(2 * k + p) * n : (2 * k + p + 1) * n] for p in range(2))
        results.append((real * (ai - bi) + imag * (ar + br), imag * (ai + bi) - real * (ar - br)))
    return results


def weights(wts, g, above):
    nr, ni = wts[g * SCALARS + 4], wts[g * SCALARS + 5]
    cr, ci = wts[g * SCALARS + 9], wts[g * SCALARS + 10]
    here = jnp.where(above, 1.0, nr), jnp.where(above, 0.0, ni)
    there = jnp.where(above, nr + cr, 1.0), jnp.where(above, ni + ci, 0.0)
    return here, there


def two_links(tab, g):
    return (tab[g * 8] >= 0) & (tab[g * 8 + 1] >= 0)


def fix_kernel(tab, wts, recv, part, slots_in, left, right, *rest, back):
    del slots_in
    if back is not None:
        prev, *rest = rest
    slots_out, token, rbuf, wbuf, pbuf, obuf, sem = rest
    count = part.shape[0]
    token[0] = 0

    @pl.loop(0, count)
    def _(g):
        @pl.when(two_links(tab, g))
        def _():
            slots = [jnp.maximum(tab[g * 8 + k], 0) for k in range(2)]
            copies = [
                pltpu.make_async_copy(recv.at[slots[k]], rbuf.at[k], sem.at[k]) for k in range(2)
            ]
            copies.append(pltpu.make_async_copy(part.at[g], pbuf, sem.at[2]))
            if back is not None:
                copies.append(pltpu.make_async_copy(prev.at[g], wbuf, sem.at[3]))
            for copy in copies:
                copy.start()
            for copy in copies:
                copy.wait()
            for k, above in enumerate((True, False)):
                here, there = weights(wts, g, above)
                x = rbuf[k, 0], rbuf[k, 1]
                if back is not None:
                    own = wbuf[0], wbuf[1]
                    (term,) = product(left[...], right[...], [own], there[:1], there[1:])
                    x = back * (x[0] + term[0]), back * (x[1] + term[1])
                (term,) = product(left[...], right[...], [x], here[:1], here[1:])
                for p in range(2):
                    obuf[1 - k, p] = pbuf[p] + term[p]
            copies = [
                pltpu.make_async_copy(obuf.at[k], slots_out.at[slots[k]], sem.at[4 + k])
                for k in range(2)
            ]
            for copy in copies:
                copy.start()
            for copy in copies:
                copy.wait()


def fix_slots(tab, wts, recv, part, slots, prev, left, right, back):
    count, _, n, _ = part.shape
    olds = [] if back is None else in_hbm(prev)
    return pl.pallas_call(
        functools.partial(fix_kernel, back=back),
        out_shape=[pltpu.HBM(slots.shape, f32), jax.ShapeDtypeStruct((1,), jnp.int32)],
        in_specs=[SMEM, SMEM, HBM, HBM, HBM, VMEM, VMEM] + [HBM] * len(olds),
        out_specs=[HBM, SMEM],
        scratch_shapes=[
            pltpu.VMEM((2, 2, n, n), f32),
            pltpu.VMEM((2, n, n), f32),
            pltpu.VMEM((2, n, n), f32),
            pltpu.VMEM((2, 2, n, n), f32),
            pltpu.SemaphoreType.DMA((6,)),
        ],
        input_output_aliases={4: 0},
        compiler_params=pltpu.CompilerParams(vmem_limit_bytes=LIMIT),
        cost_estimate=pl.CostEstimate(flops=0, bytes_accessed=1 << 10, transcendentals=0),
        name="fix_slots",
    )(tab, wts, *in_hbm(recv, part, slots), left, right, *olds)


def row_kernel(tab, wts, token, recv, part, left, right, *rest, scale, back, last):
    del token
    count, _, n, _ = part.shape
    if back is not None:
        prev, *rest = rest
    z_out, xbuf, ybuf, wbuf, zbuf, sem_x, sem_y, sem_w, sem_g, sem_z = rest

    def fetch(g, go):
        slot, low = first_slot(tab, g), tab[g * 8 + 1]
        when_copy(slot >= 0, recv.at[jnp.maximum(slot, 0)], xbuf.at[g], sem_x.at[g], go)
        when_copy(two_links(tab, g), recv.at[jnp.maximum(low, 0)], ybuf.at[g], sem_y.at[g], go)
        if go:

            @pl.when(slot < 0)
            def _():
                xbuf[g] = jnp.zeros_like(xbuf[g])

    def fetch_own(step, go):
        group = pl.ds(step * WIDTH, WIDTH)
        copies = [pltpu.make_async_copy(part.at[group], zbuf.at[group], sem_g.at[step])]
        if back is not None:
            copies.append(pltpu.make_async_copy(prev.at[group], wbuf.at[group], sem_w.at[step]))
        for copy in copies:
            copy.start() if go else copy.wait()

    def keep(step):
        group = pl.ds(step * WIDTH, WIDTH)
        return pltpu.make_async_copy(zbuf.at[group], z_out.at[group], sem_z.at[step])

    @pl.loop(0, count // WIDTH)
    def _(step):
        for k in range(WIDTH):
            fetch(step * WIDTH + k, True)
        fetch_own(step, True)

    def linked(group, buf, above):
        both = [weights(wts, g, a) for g, a in zip(group, above)]
        values = [(buf[g, 0], buf[g, 1]) for g in group]
        if back is not None:
            own = [(wbuf[g, 0], wbuf[g, 1]) for g in group]
            terms = product(
                left[...], right[...], own, [b[1][0] for b in both], [b[1][1] for b in both]
            )
            values = [
                tuple(back * (v + t) for v, t in zip(value, term))
                for value, term in zip(values, terms)
            ]
        return product(
            left[...], right[...], values, [b[0][0] for b in both], [b[0][1] for b in both]
        )

    @pl.loop(0, count // WIDTH)
    def _(step):
        group = [step * WIDTH + k for k in range(WIDTH)]
        for g in group:
            fetch(g, False)
        fetch_own(step, False)
        above = [tab[g * 8] >= 0 for g in group]
        for g, term in zip(group, linked(group, xbuf, above)):
            for p in range(2):
                if last:
                    zbuf[g, p] = zbuf[g, p] + scale * term[p]
                else:
                    zbuf[g, p] = scale * (zbuf[g, p] + term[p])
        for g in group:

            @pl.when(two_links(tab, g))
            def _():
                (term,) = linked([g], ybuf, [False])
                for p in range(2):
                    zbuf[g, p] = zbuf[g, p] + scale * term[p]

        keep(step).start()

    @pl.loop(0, count // WIDTH)
    def _(step):
        keep(step).wait()


def row_part(tab, wts, token, recv, part, prev, left, right, scale, back, last):
    count, _, n, _ = part.shape
    out = jax.ShapeDtypeStruct(part.shape, f32) if last else pltpu.HBM(part.shape, f32)
    olds = [] if back is None else in_hbm(prev)
    return pl.pallas_call(
        functools.partial(row_kernel, scale=scale, back=back, last=last),
        out_shape=out,
        in_specs=[SMEM, SMEM, SMEM, HBM, HBM, VMEM, VMEM] + [HBM] * len(olds),
        out_specs=HBM,
        scratch_shapes=[pltpu.VMEM((count, 2, n, n), f32)] * 4
        + [pltpu.SemaphoreType.DMA((count,))] * 5,
        compiler_params=pltpu.CompilerParams(vmem_limit_bytes=LIMIT),
        cost_estimate=pl.CostEstimate(
            flops=count * 64 * n * n * n, bytes_accessed=10 << 20, transcendentals=0
        ),
        name="row_part",
    )(tab, wts, token, *in_hbm(recv, part), left, right, *olds)


def local(
    densities, hamiltonian, couplings, decay_rates, correlation, upper_link, lower_link, occupation
):
    count, _, n, _ = densities.shape
    along_y, along_x = lax.axis_size("gy"), lax.axis_size("gx")
    index_x, index_y = lax.axis_index("gx"), lax.axis_index("gy")
    own = index_x * along_y + index_y
    missing = count * along_y * along_x

    row_send = pl.pallas_call(
        functools.partial(pack_rows_kernel, missing=missing, bath=2),
        out_shape=pltpu.HBM((along_y, 2, n, n), f32),
        in_specs=[SMEM, SMEM, HBM],
        out_specs=HBM,
        scratch_shapes=[pltpu.VMEM((count, 2, n, n), f32)]
        + [pltpu.SemaphoreType.DMA((count,))] * 3,
        name="pack_rows",
    )(upper_link.T, lower_link.T, densities)

    links = jnp.stack([upper_link, lower_link], axis=2)
    live = links < missing
    near = jnp.where(live[:, 0:2], links[:, 0:2] - own * count, -1).reshape(count, 4)
    rows = jnp.where(live[:, 2], (links[:, 2] // count) % along_y, -1)

    targets, usable = links[:, 3].reshape(-1), live[:, 3].reshape(-1)
    sources = jnp.repeat(jnp.arange(count, dtype=jnp.int32), 2)
    relative = (targets // count // along_y - index_x) % along_x
    same = usable[:, None] & usable[None, :] & (relative[:, None] == relative[None, :])
    start = (relative - 1) * XCAP
    recv_slot = start + jnp.any(same & (targets[None, :] < targets[:, None]), axis=1)
    send_slot = start + jnp.any(same & (sources[None, :] < sources[:, None]), axis=1)
    recv_slot = jnp.where(usable, recv_slot, -1).reshape(count, 2)
    hit = (send_slot[None, :] == jnp.arange(6, dtype=jnp.int32)[:, None]) & usable[None, :]
    ctab = jnp.max(jnp.where(hit, sources[None, :], -1), axis=1)
    tab = jnp.concatenate([rows, near, recv_slot], axis=1).reshape(-1).astype(jnp.int32)

    level = occupation.astype(f32)
    damping = jnp.sum(level * decay_rates[None, :], axis=1, keepdims=True)
    pairs = (level[:, :, None] * correlation.T[None, :, :]).reshape(count, 8)
    third = jnp.broadcast_to(correlation[:, 2][None, :], (count, 2))
    wts = jnp.concatenate([pairs, damping, third], axis=1).reshape(-1)

    mats = lambda rows, cols: jax.ShapeDtypeStruct((rows, cols), bf16)
    left, right, row_left, row_right = pl.pallas_call(
        prepare_kernel,
        out_shape=[mats(2 * n, 10 * n), mats(10 * n, 2 * n), mats(2 * n, 2 * n), mats(2 * n, 2 * n)],
        in_specs=[VMEM, VMEM],
        out_specs=[VMEM] * 4,
        name="prepare",
    )(hamiltonian, couplings)

    exchange = lambda a: lax.all_to_all(a, "gy", split_axis=0, concat_axis=0, tiled=True)
    states, acc, parts = [densities], None, None
    token = jnp.zeros((1,), jnp.int32)
    recv = exchange(row_send)
    for level in range(4):
        z, last = states[level], level == 3
        col_send = pack_columns(ctab, z)
        arrived = [
            lax.ppermute(col_send[s - 1], "gx", [(x, (x + s) % along_x) for x in range(along_x)])
            for s in range(1, along_x)
        ]
        scale = step_size / (level + 1)
        parts = local_part(
            tab, wts, z, arrived[::-1], left, right, acc, along_y, scale if last else None
        )
        acc = densities if level == 0 else None if last else parts[2]
        back = step_size / level if level else None
        prev = states[level - 1] if level else None
        mats = (row_left, row_right)
        if not last:
            slots, token = fix_slots(tab, wts, recv, parts[0], parts[1], prev, *mats, back)
            following = exchange(slots)
        new = row_part(tab, wts, token, recv, parts[0], prev, *mats, scale, back, last)
        if last:
            return new
        states.append(new)
        recv = following


def solution(mesh):
    return jax.shard_map(
        local,
        mesh=mesh,
        in_specs=(
            P(("gx", "gy"), None, None, None),
            P(),
            P(),
            P(),
            P(),
            P(("gx", "gy"), None),
            P(("gx", "gy"), None),
            P(("gx", "gy"), None),
        ),
        out_specs=P(("gx", "gy"), None, None, None),
        check_vma=False,
    )
```

```python
import functools

import jax
import jax.numpy as jnp
from jax import lax
from jax.experimental import pallas as pl
from jax.experimental.pallas import tpu as pltpu
from jax.sharding import PartitionSpec as P

XCAP = 2
step_size = 0.1
f32, bf16 = jnp.float32, jnp.bfloat16
LIMIT = 24 << 20
WIDTH = 4
SCALARS = 11
HBM = pl.BlockSpec(memory_space=pltpu.HBM)
SMEM = pl.BlockSpec(memory_space=pltpu.SMEM)
VMEM = pl.BlockSpec(memory_space=pltpu.VMEM)


def split(value):
    high = value.astype(bf16)
    return high, (value - high.astype(f32)).astype(bf16)


def prepare_kernel(h_ref, v_ref, left_ref, right_ref, row_left_ref, row_right_ref):
    n = h_ref.shape[-1]

    def put(matrix, left, right, place):
        high, low = split(matrix)
        start = place * 2 * n
        for half in range(2):
            cols = slice(start + half * n, start + (half + 1) * n)
            left[0:n, cols] = high
            left[n : 2 * n, cols] = low
            right[cols, 0:n] = high
            right[cols, n : 2 * n] = low

    terms = [h_ref[1], h_ref[0], v_ref[0], v_ref[1], v_ref[3]]
    for place, matrix in enumerate(terms):
        put(matrix, left_ref, right_ref, place)
    put(v_ref[2], row_left_ref, row_right_ref, 0)


def sandwich(terms, left, right):
    n = terms[0][0][0].shape[-1]
    columns, rows = [], []
    for (la, lb), (ra, rb) in terms:
        columns += [jnp.concatenate(pair, axis=1) for pair in zip(split(la), split(lb))]
        rows += [jnp.concatenate(pair, axis=0) for pair in zip(split(ra), split(rb))]
    stacked = jnp.concatenate(columns, axis=0)
    beside = jnp.concatenate(rows, axis=1)
    ahead = jnp.dot(left, stacked, preferred_element_type=f32)
    behind = jnp.dot(beside, right, preferred_element_type=f32)
    ahead = ahead[0:n] + ahead[n:]
    behind = behind[:, 0:n] + behind[:, n:]
    return ahead[:, 0:n] - behind[0:n], ahead[:, n:] - behind[n:]


def bath_term(ur, ui, lr, li, wr, wi):
    arr, ari, air, aii = wr * lr, wi * lr, wr * li, wi * li
    real, imag = ur + arr, ui + air
    return ((imag + ari, aii - real), (imag - ari, -real - aii))


def first_slot(tab, g):
    up, low = tab[g * 8], tab[g * 8 + 1]
    return jnp.where(up >= 0, up, low)


def when_copy(live, source, target, sem, go):
    @pl.when(live)
    def _():
        copy = pltpu.make_async_copy(source, target, sem)
        copy.start() if go else copy.wait()


def send_slots(tab, g, buf, row_out, sem_u, sem_l, go):
    for k, sem in ((0, sem_u), (1, sem_l)):
        slot = tab[g * 8 + k]
        when_copy(slot >= 0, buf.at[g], row_out.at[jnp.maximum(slot, 0)], sem.at[g], go)


def local_kernel(tab, wts, z_ref, c1, c2, c3, left, right, *rest, with_sum, last_scale):
    count = z_ref.shape[0]
    if with_sum:
        acc_ref, *rest = rest
    last = last_scale is not None
    keep_sum = with_sum and not last
    out_ref, *rest = rest
    if not last:
        row_out, *rest = rest
    if keep_sum:
        sum_ref, *rest = rest
    cbuf, sems, sem_u, sem_l = rest

    copies = [
        pltpu.make_async_copy(c, cbuf.at[pl.ds(XCAP * k, XCAP)], sems.at[k])
        for k, c in enumerate((c1, c2, c3))
    ]
    for copy in copies:
        copy.start()
    for copy in copies:
        copy.wait()

    def one(g):
        yr, yi = z_ref[g, 0], z_ref[g, 1]
        terms = [((yr, yi), (yr, yi)), ((yi, -yr), (yi, -yr))]
        for k, (ref, bath) in enumerate(((z_ref, 0), (z_ref, 1), (cbuf, 3))):
            up, low = tab[g * 8 + 2 + 2 * k], tab[g * 8 + 3 + 2 * k]
            u, l = jnp.maximum(up, 0), jnp.maximum(low, 0)
            ur, ui = (jnp.where(up >= 0, ref[u, part], 0.0) for part in range(2))
            lr, li = (jnp.where(low >= 0, ref[l, part], 0.0) for part in range(2))
            wr, wi = wts[g * SCALARS + 2 * bath], wts[g * SCALARS + 2 * bath + 1]
            terms.append(bath_term(ur, ui, lr, li, wr, wi))
        out_r, out_i = sandwich(terms, left[...], right[...])
        damp = wts[g * SCALARS + 8]
        out_r, out_i = out_r - damp * yr, out_i - damp * yi
        if with_sum:
            sum_r, sum_i = acc_ref[g, 0] + yr, acc_ref[g, 1] + yi
        if last_scale is not None:
            out_r, out_i = sum_r + last_scale * out_r, sum_i + last_scale * out_i
        out_ref[g, 0], out_ref[g, 1] = out_r, out_i
        if keep_sum:
            sum_ref[g, 0], sum_ref[g, 1] = sum_r, sum_i

    width = 2

    @pl.loop(0, count // width)
    def _(step):
        for k in range(width):
            one(step * width + k)
        if not last:
            for k in range(width):
                send_slots(tab, step * width + k, out_ref, row_out, sem_u, sem_l, True)

    if not last:

        @pl.loop(0, count)
        def _(g):
            send_slots(tab, g, out_ref, row_out, sem_u, sem_l, False)


def in_hbm(*arrays):
    return [pltpu.with_memory_space_constraint(a, pltpu.HBM) for a in arrays]


def local_part(tab, wts, z, cols, left, right, acc, slots, last_scale):
    count, _, n, _ = z.shape
    with_sum, last = acc is not None, last_scale is not None
    outs, places = [jax.ShapeDtypeStruct(z.shape, f32)], [VMEM]
    if not last:
        outs, places = outs + [pltpu.HBM((slots, 2, n, n), f32)], places + [HBM]
    if with_sum and not last:
        outs, places = outs + [jax.ShapeDtypeStruct(z.shape, f32)], places + [VMEM]
    return pl.pallas_call(
        functools.partial(local_kernel, with_sum=with_sum, last_scale=last_scale),
        out_shape=outs,
        in_specs=[SMEM, SMEM, VMEM, HBM, HBM, HBM, VMEM, VMEM] + [VMEM] * with_sum,
        out_specs=places,
        scratch_shapes=[
            pltpu.VMEM((3 * XCAP, 2, n, n), f32),
            pltpu.SemaphoreType.DMA((3,)),
            pltpu.SemaphoreType.DMA((count,)),
            pltpu.SemaphoreType.DMA((count,)),
        ],
        compiler_params=pltpu.CompilerParams(vmem_limit_bytes=LIMIT),
        cost_estimate=pl.CostEstimate(
            flops=count * 160 * n * n * n, bytes_accessed=8 << 20, transcendentals=0
        ),
        name="local_part",
    )(tab, wts, z, *cols, left, right, *([acc] if with_sum else []))


def pack_columns_kernel(ctab, z_ref, o1, o2, o3, buf, sem):
    outs = (o1, o2, o3)
    slots = len(outs) * XCAP
    for go in (True, False):
        for k in range(slots):
            g = ctab[k]
            when_copy(g >= 0, z_ref.at[jnp.maximum(g, 0)], buf.at[k], sem.at[k], go)
    for go in (True, False):
        for k in range(slots):
            when_copy(ctab[k] >= 0, buf.at[k], outs[k // XCAP].at[k % XCAP], sem.at[k], go)


def pack_columns(ctab, z):
    count, _, n, _ = z.shape
    return pl.pallas_call(
        pack_columns_kernel,
        out_shape=[pltpu.HBM((XCAP, 2, n, n), f32)] * 3,
        in_specs=[SMEM, HBM],
        out_specs=[HBM] * 3,
        scratch_shapes=[
            pltpu.VMEM((3 * XCAP, 2, n, n), f32),
            pltpu.SemaphoreType.DMA((3 * XCAP,)),
        ],
        cost_estimate=pl.CostEstimate(flops=0, bytes_accessed=1 << 20, transcendentals=0),
        name="pack_columns",
    )(ctab, *in_hbm(z))


def pack_rows_kernel(up_ref, low_ref, z_ref, row_out, buf, sem_in, sem_u, sem_l, *, missing, bath):
    count, along_y = z_ref.shape[0], row_out.shape[0]
    links = ((up_ref, sem_u), (low_ref, sem_l))

    def load(g, go):
        linked = (up_ref[bath, g] < missing) | (low_ref[bath, g] < missing)
        when_copy(linked, z_ref.at[g], buf.at[g], sem_in.at[g], go)

    def send(g, go):
        for ref, sem in links:
            target = ref[bath, g]
            slot = lax.rem(lax.div(target, count), along_y)
            when_copy(target < missing, buf.at[g], row_out.at[slot], sem.at[g], go)

    @pl.loop(0, count)
    def _(g):
        load(g, True)

    @pl.loop(0, count)
    def _(g):
        load(g, False)
        send(g, True)

    @pl.loop(0, count)
    def _(g):
        send(g, False)


def product(left, right, values, reals, imags):
    n = values[0][0].shape[-1]
    ahead, beside = [], []
    for xr, xi in values:
        (hr, tr), (hi, ti) = split(xr), split(xi)
        high, tail = jnp.concatenate([hr, hi], 1), jnp.concatenate([tr, ti], 1)
        rows = jnp.dot(left, jnp.concatenate([high, tail], 0), preferred_element_type=f32)
        ahead.append(rows[0:n] + rows[n:])
        beside.append(jnp.concatenate([hr, tr], 1))
        beside.append(jnp.concatenate([hi, ti], 1))
    behind = jnp.dot(jnp.concatenate(beside, 0), right, preferred_element_type=f32)
    behind = behind[:, 0:n] + behind[:, n:]
    results = []
    for k, (real, imag) in enumerate(zip(reals, imags)):
        ar, ai = ahead[k][:, 0:n], ahead[k][:, n:]
        br, bi = (behind[(2 * k + p) * n : (2 * k + p + 1) * n] for p in range(2))
        results.append((real * (ai - bi) + imag * (ar + br), imag * (ai + bi) - real * (ar - br)))
    return results


def weights(wts, g, above):
    nr, ni = wts[g * SCALARS + 4], wts[g * SCALARS + 5]
    cr, ci = wts[g * SCALARS + 9], wts[g * SCALARS + 10]
    here = jnp.where(above, 1.0, nr), jnp.where(above, 0.0, ni)
    there = jnp.where(above, nr + cr, 1.0), jnp.where(above, ni + ci, 0.0)
    return here, there


def two_links(tab, g):
    return (tab[g * 8] >= 0) & (tab[g * 8 + 1] >= 0)


def fix_kernel(tab, wts, recv, part, slots_in, left, right, *rest, back):
    del slots_in
    if back is not None:
        prev, *rest = rest
    slots_out, token, rbuf, wbuf, pbuf, obuf, sem = rest
    count = part.shape[0]
    token[0] = 0

    @pl.loop(0, count)
    def _(g):
        @pl.when(two_links(tab, g))
        def _():
            slots = [jnp.maximum(tab[g * 8 + k], 0) for k in range(2)]
            copies = [
                pltpu.make_async_copy(recv.at[slots[k]], rbuf.at[k], sem.at[k]) for k in range(2)
            ]
            copies.append(pltpu.make_async_copy(part.at[g], pbuf, sem.at[2]))
            if back is not None:
                copies.append(pltpu.make_async_copy(prev.at[g], wbuf, sem.at[3]))
            for copy in copies:
                copy.start()
            for copy in copies:
                copy.wait()
            for k, above in enumerate((True, False)):
                here, there = weights(wts, g, above)
                x = rbuf[k, 0], rbuf[k, 1]
                if back is not None:
                    own = wbuf[0], wbuf[1]
                    (term,) = product(left[...], right[...], [own], there[:1], there[1:])
                    x = back * (x[0] + term[0]), back * (x[1] + term[1])
                (term,) = product(left[...], right[...], [x], here[:1], here[1:])
                for p in range(2):
                    obuf[1 - k, p] = pbuf[p] + term[p]
            copies = [
                pltpu.make_async_copy(obuf.at[k], slots_out.at[slots[k]], sem.at[4 + k])
                for k in range(2)
            ]
            for copy in copies:
                copy.start()
            for copy in copies:
                copy.wait()


def fix_slots(tab, wts, recv, part, slots, prev, left, right, back):
    count, _, n, _ = part.shape
    olds = [] if back is None else in_hbm(prev)
    return pl.pallas_call(
        functools.partial(fix_kernel, back=back),
        out_shape=[pltpu.HBM(slots.shape, f32), jax.ShapeDtypeStruct((1,), jnp.int32)],
        in_specs=[SMEM, SMEM, HBM, HBM, HBM, VMEM, VMEM] + [HBM] * len(olds),
        out_specs=[HBM, SMEM],
        scratch_shapes=[
            pltpu.VMEM((2, 2, n, n), f32),
            pltpu.VMEM((2, n, n), f32),
            pltpu.VMEM((2, n, n), f32),
            pltpu.VMEM((2, 2, n, n), f32),
            pltpu.SemaphoreType.DMA((6,)),
        ],
        input_output_aliases={4: 0},
        compiler_params=pltpu.CompilerParams(vmem_limit_bytes=LIMIT),
        cost_estimate=pl.CostEstimate(flops=0, bytes_accessed=1 << 10, transcendentals=0),
        name="fix_slots",
    )(tab, wts, *in_hbm(recv, part, slots), left, right, *olds)


def row_kernel(tab, wts, token, recv, part, left, right, *rest, scale, back, last, own_only):
    del token
    count, _, n, _ = part.shape
    if back is not None:
        prev, *rest = rest
    z_out, xbuf, ybuf, wbuf, zbuf, sem_x, sem_y, sem_w, sem_g, sem_z = rest

    def fetch(g, go):
        if own_only:
            return
        slot, low = first_slot(tab, g), tab[g * 8 + 1]
        when_copy(slot >= 0, recv.at[jnp.maximum(slot, 0)], xbuf.at[g], sem_x.at[g], go)
        when_copy(two_links(tab, g), recv.at[jnp.maximum(low, 0)], ybuf.at[g], sem_y.at[g], go)
        if go:

            @pl.when(slot < 0)
            def _():
                xbuf[g] = jnp.zeros_like(xbuf[g])

    def fetch_own(step, go):
        group = pl.ds(step * WIDTH, WIDTH)
        copies = [pltpu.make_async_copy(part.at[group], zbuf.at[group], sem_g.at[step])]
        if back is not None:
            copies.append(pltpu.make_async_copy(prev.at[group], wbuf.at[group], sem_w.at[step]))
        for copy in copies:
            copy.start() if go else copy.wait()

    def keep(step):
        group = pl.ds(step * WIDTH, WIDTH)
        return pltpu.make_async_copy(zbuf.at[group], z_out.at[group], sem_z.at[step])

    @pl.loop(0, count // WIDTH)
    def _(step):
        for k in range(WIDTH):
            fetch(step * WIDTH + k, True)
        fetch_own(step, True)

    def linked(group, buf, above):
        both = [weights(wts, g, a) for g, a in zip(group, above)]
        values = [(0.0, 0.0) if own_only else (buf[g, 0], buf[g, 1]) for g in group]
        if back is not None:
            own = [(wbuf[g, 0], wbuf[g, 1]) for g in group]
            terms = product(
                left[...], right[...], own, [b[1][0] for b in both], [b[1][1] for b in both]
            )
            values = [
                tuple(back * (v + t) for v, t in zip(value, term))
                for value, term in zip(values, terms)
            ]
        return product(
            left[...], right[...], values, [b[0][0] for b in both], [b[0][1] for b in both]
        )

    @pl.loop(0, count // WIDTH)
    def _(step):
        group = [step * WIDTH + k for k in range(WIDTH)]
        for g in group:
            fetch(g, False)
        fetch_own(step, False)
        above = [tab[g * 8] >= 0 for g in group]
        for g, term in zip(group, linked(group, xbuf, above)):
            for p in range(2):
                if last:
                    zbuf[g, p] = zbuf[g, p] + scale * term[p]
                else:
                    zbuf[g, p] = scale * (zbuf[g, p] + term[p])
        for g in group:

            @pl.when(two_links(tab, g))
            def _():
                (term,) = linked([g], ybuf, [False])
                for p in range(2):
                    zbuf[g, p] = zbuf[g, p] + scale * term[p]

        keep(step).start()

    @pl.loop(0, count // WIDTH)
    def _(step):
        keep(step).wait()


def row_part(tab, wts, token, recv, part, prev, left, right, scale, back, last, own_only=False):
    count, _, n, _ = part.shape
    out = jax.ShapeDtypeStruct(part.shape, f32) if last else pltpu.HBM(part.shape, f32)
    olds = [] if back is None else in_hbm(prev)
    return pl.pallas_call(
        functools.partial(row_kernel, scale=scale, back=back, last=last, own_only=own_only),
        out_shape=out,
        in_specs=[SMEM, SMEM, SMEM, HBM, HBM, VMEM, VMEM] + [HBM] * len(olds),
        out_specs=HBM,
        scratch_shapes=[pltpu.VMEM((count, 2, n, n), f32)] * 4
        + [pltpu.SemaphoreType.DMA((count,))] * 5,
        compiler_params=pltpu.CompilerParams(vmem_limit_bytes=LIMIT),
        cost_estimate=pl.CostEstimate(
            flops=count * 64 * n * n * n, bytes_accessed=10 << 20, transcendentals=0
        ),
        name="row_part",
    )(tab, wts, token, *in_hbm(recv, part), left, right, *olds)


def local(
    densities, hamiltonian, couplings, decay_rates, correlation, upper_link, lower_link, occupation
):
    count, _, n, _ = densities.shape
    along_y, along_x = lax.axis_size("gy"), lax.axis_size("gx")
    index_x, index_y = lax.axis_index("gx"), lax.axis_index("gy")
    own = index_x * along_y + index_y
    missing = count * along_y * along_x

    row_send = pl.pallas_call(
        functools.partial(pack_rows_kernel, missing=missing, bath=2),
        out_shape=pltpu.HBM((along_y, 2, n, n), f32),
        in_specs=[SMEM, SMEM, HBM],
        out_specs=HBM,
        scratch_shapes=[pltpu.VMEM((count, 2, n, n), f32)]
        + [pltpu.SemaphoreType.DMA((count,))] * 3,
        name="pack_rows",
    )(upper_link.T, lower_link.T, densities)

    links = jnp.stack([upper_link, lower_link], axis=2)
    live = links < missing
    near = jnp.where(live[:, 0:2], links[:, 0:2] - own * count, -1).reshape(count, 4)
    rows = jnp.where(live[:, 2], (links[:, 2] // count) % along_y, -1)

    targets, usable = links[:, 3].reshape(-1), live[:, 3].reshape(-1)
    sources = jnp.repeat(jnp.arange(count, dtype=jnp.int32), 2)
    relative = (targets // count // along_y - index_x) % along_x
    same = usable[:, None] & usable[None, :] & (relative[:, None] == relative[None, :])
    start = (relative - 1) * XCAP
    recv_slot = start + jnp.any(same & (targets[None, :] < targets[:, None]), axis=1)
    send_slot = start + jnp.any(same & (sources[None, :] < sources[:, None]), axis=1)
    recv_slot = jnp.where(usable, recv_slot, -1).reshape(count, 2)
    hit = (send_slot[None, :] == jnp.arange(6, dtype=jnp.int32)[:, None]) & usable[None, :]
    ctab = jnp.max(jnp.where(hit, sources[None, :], -1), axis=1)
    tab = jnp.concatenate([rows, near, recv_slot], axis=1).reshape(-1).astype(jnp.int32)

    level = occupation.astype(f32)
    damping = jnp.sum(level * decay_rates[None, :], axis=1, keepdims=True)
    pairs = (level[:, :, None] * correlation.T[None, :, :]).reshape(count, 8)
    third = jnp.broadcast_to(correlation[:, 2][None, :], (count, 2))
    wts = jnp.concatenate([pairs, damping, third], axis=1).reshape(-1)

    mats = lambda rows, cols: jax.ShapeDtypeStruct((rows, cols), bf16)
    left, right, row_left, row_right = pl.pallas_call(
        prepare_kernel,
        out_shape=[mats(2 * n, 10 * n), mats(10 * n, 2 * n), mats(2 * n, 2 * n), mats(2 * n, 2 * n)],
        in_specs=[VMEM, VMEM],
        out_specs=[VMEM] * 4,
        name="prepare",
    )(hamiltonian, couplings)

    exchange = lambda a: lax.all_to_all(a, "gy", split_axis=0, concat_axis=0, tiled=True)
    states, acc, parts = [densities], None, None
    token = jnp.zeros((1,), jnp.int32)
    recv = exchange(row_send)
    for level in range(4):
        z, last = states[level], level == 3
        col_send = pack_columns(ctab, z)
        arrived = [
            lax.ppermute(col_send[s - 1], "gx", [(x, (x + s) % along_x) for x in range(along_x)])
            for s in range(1, along_x)
        ]
        scale = step_size / (level + 1)
        back = step_size / level if level else None
        prev = states[level - 1] if level else None
        mats = (row_left, row_right)
        if last:
            acc = row_part(tab, wts, token, prev, acc, prev, *mats, scale, back, True, own_only=True)
            scale_row, back = scale * back, None
        else:
            scale_row = scale
        parts = local_part(
            tab, wts, z, arrived[::-1], left, right, acc, along_y, scale if last else None
        )
        acc = densities if level == 0 else None if last else parts[2]
        if not last:
            slots, token = fix_slots(tab, wts, recv, parts[0], parts[1], prev, *mats, back)
            following = exchange(slots)
        new = row_part(tab, wts, token, recv, parts[0], prev, *mats, scale_row, back, last)
        if last:
            return new
        states.append(new)
        recv = following


def solution(mesh):
    return jax.shard_map(
        local,
        mesh=mesh,
        in_specs=(
            P(("gx", "gy"), None, None, None),
            P(),
            P(),
            P(),
            P(),
            P(("gx", "gy"), None),
            P(("gx", "gy"), None),
            P(("gx", "gy"), None),
        ),
        out_specs=P(("gx", "gy"), None, None, None),
        check_vma=False,
    )
```

```python
import functools

import jax
import jax.numpy as jnp
from jax import lax
from jax.experimental import pallas as pl
from jax.experimental.pallas import tpu as pltpu
from jax.sharding import PartitionSpec as P

XCAP = 2
step_size = 0.1
f32, bf16 = jnp.float32, jnp.bfloat16
LIMIT = 24 << 20
WIDTH = 4
SCALARS = 11
HBM = pl.BlockSpec(memory_space=pltpu.HBM)
SMEM = pl.BlockSpec(memory_space=pltpu.SMEM)
VMEM = pl.BlockSpec(memory_space=pltpu.VMEM)


def split(value):
    high = value.astype(bf16)
    return high, (value - high.astype(f32)).astype(bf16)


def prepare_kernel(h_ref, v_ref, left_ref, right_ref, row_left_ref, row_right_ref):
    n = h_ref.shape[-1]

    def put(matrix, left, right, place):
        high, low = split(matrix)
        start = place * 2 * n
        for half in range(2):
            cols = slice(start + half * n, start + (half + 1) * n)
            left[0:n, cols] = high
            left[n : 2 * n, cols] = low
            right[cols, 0:n] = high
            right[cols, n : 2 * n] = low

    terms = [h_ref[1], h_ref[0], v_ref[0], v_ref[1], v_ref[3]]
    for place, matrix in enumerate(terms):
        put(matrix, left_ref, right_ref, place)
    put(v_ref[2], row_left_ref, row_right_ref, 0)


def sandwich(terms, left, right):
    n = terms[0][0][0].shape[-1]
    columns, rows = [], []
    for (la, lb), (ra, rb) in terms:
        columns += [jnp.concatenate(pair, axis=1) for pair in zip(split(la), split(lb))]
        rows += [jnp.concatenate(pair, axis=0) for pair in zip(split(ra), split(rb))]
    stacked = jnp.concatenate(columns, axis=0)
    beside = jnp.concatenate(rows, axis=1)
    ahead = jnp.dot(left, stacked, preferred_element_type=f32)
    behind = jnp.dot(beside, right, preferred_element_type=f32)
    ahead = ahead[0:n] + ahead[n:]
    behind = behind[:, 0:n] + behind[:, n:]
    return ahead[:, 0:n] - behind[0:n], ahead[:, n:] - behind[n:]


def bath_term(ur, ui, lr, li, wr, wi):
    arr, ari, air, aii = wr * lr, wi * lr, wr * li, wi * li
    real, imag = ur + arr, ui + air
    return ((imag + ari, aii - real), (imag - ari, -real - aii))


def first_slot(tab, g):
    up, low = tab[g * 8], tab[g * 8 + 1]
    return jnp.where(up >= 0, up, low)


def when_copy(live, source, target, sem, go):
    @pl.when(live)
    def _():
        copy = pltpu.make_async_copy(source, target, sem)
        copy.start() if go else copy.wait()


def send_slots(tab, g, buf, row_out, sem_u, sem_l, go):
    for k, sem in ((0, sem_u), (1, sem_l)):
        slot = tab[g * 8 + k]
        when_copy(slot >= 0, buf.at[g], row_out.at[jnp.maximum(slot, 0)], sem.at[g], go)


def local_kernel(tab, wts, z_ref, c1, c2, c3, left, right, *rest, with_sum, last_scale):
    count = z_ref.shape[0]
    if with_sum:
        acc_ref, *rest = rest
    last = last_scale is not None
    keep_sum = with_sum and not last
    out_ref, *rest = rest
    if not last:
        row_out, *rest = rest
    if keep_sum:
        sum_ref, *rest = rest
    cbuf, sems, sem_u, sem_l = rest

    copies = [
        pltpu.make_async_copy(c, cbuf.at[pl.ds(XCAP * k, XCAP)], sems.at[k])
        for k, c in enumerate((c1, c2, c3))
    ]
    for copy in copies:
        copy.start()
    for copy in copies:
        copy.wait()

    def one(g):
        yr, yi = z_ref[g, 0], z_ref[g, 1]
        terms = [((yr, yi), (yr, yi)), ((yi, -yr), (yi, -yr))]
        for k, (ref, bath) in enumerate(((z_ref, 0), (z_ref, 1), (cbuf, 3))):
            up, low = tab[g * 8 + 2 + 2 * k], tab[g * 8 + 3 + 2 * k]
            u, l = jnp.maximum(up, 0), jnp.maximum(low, 0)
            ur, ui = (jnp.where(up >= 0, ref[u, part], 0.0) for part in range(2))
            lr, li = (jnp.where(low >= 0, ref[l, part], 0.0) for part in range(2))
            wr, wi = wts[g * SCALARS + 2 * bath], wts[g * SCALARS + 2 * bath + 1]
            terms.append(bath_term(ur, ui, lr, li, wr, wi))
        out_r, out_i = sandwich(terms, left[...], right[...])
        damp = wts[g * SCALARS + 8]
        out_r, out_i = out_r - damp * yr, out_i - damp * yi
        if with_sum:
            sum_r, sum_i = acc_ref[g, 0] + yr, acc_ref[g, 1] + yi
        if last_scale is not None:
            out_r, out_i = sum_r + last_scale * out_r, sum_i + last_scale * out_i
        out_ref[g, 0], out_ref[g, 1] = out_r, out_i
        if keep_sum:
            sum_ref[g, 0], sum_ref[g, 1] = sum_r, sum_i

    width = 2

    @pl.loop(0, count // width)
    def _(step):
        for k in range(width):
            one(step * width + k)
        if not last:
            for k in range(width):
                send_slots(tab, step * width + k, out_ref, row_out, sem_u, sem_l, True)

    if not last:

        @pl.loop(0, count)
        def _(g):
            send_slots(tab, g, out_ref, row_out, sem_u, sem_l, False)


def in_hbm(*arrays):
    return [pltpu.with_memory_space_constraint(a, pltpu.HBM) for a in arrays]


def local_part(tab, wts, z, cols, left, right, acc, slots, last_scale):
    count, _, n, _ = z.shape
    with_sum, last = acc is not None, last_scale is not None
    outs, places = [jax.ShapeDtypeStruct(z.shape, f32)], [VMEM]
    if not last:
        outs, places = outs + [pltpu.HBM((slots, 2, n, n), f32)], places + [HBM]
    if with_sum and not last:
        outs, places = outs + [jax.ShapeDtypeStruct(z.shape, f32)], places + [VMEM]
    return pl.pallas_call(
        functools.partial(local_kernel, with_sum=with_sum, last_scale=last_scale),
        out_shape=outs,
        in_specs=[SMEM, SMEM, VMEM, HBM, HBM, HBM, VMEM, VMEM] + [VMEM] * with_sum,
        out_specs=places,
        scratch_shapes=[
            pltpu.VMEM((3 * XCAP, 2, n, n), f32),
            pltpu.SemaphoreType.DMA((3,)),
            pltpu.SemaphoreType.DMA((count,)),
            pltpu.SemaphoreType.DMA((count,)),
        ],
        compiler_params=pltpu.CompilerParams(vmem_limit_bytes=LIMIT),
        cost_estimate=pl.CostEstimate(
            flops=count * 160 * n * n * n, bytes_accessed=8 << 20, transcendentals=0
        ),
        name="local_part",
    )(tab, wts, z, *cols, left, right, *([acc] if with_sum else []))


def pack_columns_kernel(ctab, z_ref, o1, o2, o3, buf, sem):
    outs = (o1, o2, o3)
    slots = len(outs) * XCAP
    for go in (True, False):
        for k in range(slots):
            g = ctab[k]
            when_copy(g >= 0, z_ref.at[jnp.maximum(g, 0)], buf.at[k], sem.at[k], go)
    for go in (True, False):
        for k in range(slots):
            when_copy(ctab[k] >= 0, buf.at[k], outs[k // XCAP].at[k % XCAP], sem.at[k], go)


def pack_columns(ctab, z):
    count, _, n, _ = z.shape
    return pl.pallas_call(
        pack_columns_kernel,
        out_shape=[pltpu.HBM((XCAP, 2, n, n), f32)] * 3,
        in_specs=[SMEM, HBM],
        out_specs=[HBM] * 3,
        scratch_shapes=[
            pltpu.VMEM((3 * XCAP, 2, n, n), f32),
            pltpu.SemaphoreType.DMA((3 * XCAP,)),
        ],
        cost_estimate=pl.CostEstimate(flops=0, bytes_accessed=1 << 20, transcendentals=0),
        name="pack_columns",
    )(ctab, *in_hbm(z))


def pack_rows_kernel(up_ref, low_ref, z_ref, row_out, buf, sem_in, sem_u, sem_l, *, missing, bath):
    count, along_y = z_ref.shape[0], row_out.shape[0]
    links = ((up_ref, sem_u), (low_ref, sem_l))

    def load(g, go):
        linked = (up_ref[bath, g] < missing) | (low_ref[bath, g] < missing)
        when_copy(linked, z_ref.at[g], buf.at[g], sem_in.at[g], go)

    def send(g, go):
        for ref, sem in links:
            target = ref[bath, g]
            slot = lax.rem(lax.div(target, count), along_y)
            when_copy(target < missing, buf.at[g], row_out.at[slot], sem.at[g], go)

    @pl.loop(0, count)
    def _(g):
        load(g, True)

    @pl.loop(0, count)
    def _(g):
        load(g, False)
        send(g, True)

    @pl.loop(0, count)
    def _(g):
        send(g, False)


def product(left, right, values, reals, imags):
    n = values[0][0].shape[-1]
    ahead, beside = [], []
    for xr, xi in values:
        (hr, tr), (hi, ti) = split(xr), split(xi)
        high, tail = jnp.concatenate([hr, hi], 1), jnp.concatenate([tr, ti], 1)
        rows = jnp.dot(left, jnp.concatenate([high, tail], 0), preferred_element_type=f32)
        ahead.append(rows[0:n] + rows[n:])
        beside.append(jnp.concatenate([hr, tr], 1))
        beside.append(jnp.concatenate([hi, ti], 1))
    behind = jnp.dot(jnp.concatenate(beside, 0), right, preferred_element_type=f32)
    behind = behind[:, 0:n] + behind[:, n:]
    results = []
    for k, (real, imag) in enumerate(zip(reals, imags)):
        ar, ai = ahead[k][:, 0:n], ahead[k][:, n:]
        br, bi = (behind[(2 * k + p) * n : (2 * k + p + 1) * n] for p in range(2))
        results.append((real * (ai - bi) + imag * (ar + br), imag * (ai + bi) - real * (ar - br)))
    return results


def weights(wts, g, above):
    nr, ni = wts[g * SCALARS + 4], wts[g * SCALARS + 5]
    cr, ci = wts[g * SCALARS + 9], wts[g * SCALARS + 10]
    here = jnp.where(above, 1.0, nr), jnp.where(above, 0.0, ni)
    there = jnp.where(above, nr + cr, 1.0), jnp.where(above, ni + ci, 0.0)
    return here, there


def two_links(tab, g):
    return (tab[g * 8] >= 0) & (tab[g * 8 + 1] >= 0)


def fix_kernel(tab, wts, recv, part, slots_in, left, right, *rest, back):
    del slots_in
    if back is not None:
        prev, *rest = rest
    slots_out, token, rbuf, wbuf, pbuf, obuf, sem = rest
    count = part.shape[0]
    token[0] = 0

    @pl.loop(0, count)
    def _(g):
        @pl.when(two_links(tab, g))
        def _():
            slots = [jnp.maximum(tab[g * 8 + k], 0) for k in range(2)]
            copies = [
                pltpu.make_async_copy(recv.at[slots[k]], rbuf.at[k], sem.at[k]) for k in range(2)
            ]
            copies.append(pltpu.make_async_copy(part.at[g], pbuf, sem.at[2]))
            if back is not None:
                copies.append(pltpu.make_async_copy(prev.at[g], wbuf, sem.at[3]))
            for copy in copies:
                copy.start()
            for copy in copies:
                copy.wait()
            for k, above in enumerate((True, False)):
                here, there = weights(wts, g, above)
                x = rbuf[k, 0], rbuf[k, 1]
                if back is not None:
                    own = wbuf[0], wbuf[1]
                    (term,) = product(left[...], right[...], [own], there[:1], there[1:])
                    x = back * (x[0] + term[0]), back * (x[1] + term[1])
                (term,) = product(left[...], right[...], [x], here[:1], here[1:])
                for p in range(2):
                    obuf[1 - k, p] = pbuf[p] + term[p]
            copies = [
                pltpu.make_async_copy(obuf.at[k], slots_out.at[slots[k]], sem.at[4 + k])
                for k in range(2)
            ]
            for copy in copies:
                copy.start()
            for copy in copies:
                copy.wait()


def fix_slots(tab, wts, recv, part, slots, prev, left, right, back):
    count, _, n, _ = part.shape
    olds = [] if back is None else in_hbm(prev)
    return pl.pallas_call(
        functools.partial(fix_kernel, back=back),
        out_shape=[pltpu.HBM(slots.shape, f32), jax.ShapeDtypeStruct((1,), jnp.int32)],
        in_specs=[SMEM, SMEM, HBM, HBM, HBM, VMEM, VMEM] + [HBM] * len(olds),
        out_specs=[HBM, SMEM],
        scratch_shapes=[
            pltpu.VMEM((2, 2, n, n), f32),
            pltpu.VMEM((2, n, n), f32),
            pltpu.VMEM((2, n, n), f32),
            pltpu.VMEM((2, 2, n, n), f32),
            pltpu.SemaphoreType.DMA((6,)),
        ],
        input_output_aliases={4: 0},
        compiler_params=pltpu.CompilerParams(vmem_limit_bytes=LIMIT),
        cost_estimate=pl.CostEstimate(flops=0, bytes_accessed=1 << 10, transcendentals=0),
        name="fix_slots",
    )(tab, wts, *in_hbm(recv, part, slots), left, right, *olds)


def row_kernel(tab, wts, token, recv, part, left, right, *rest, scale, back, last, own_only):
    del token
    count, _, n, _ = part.shape
    if back is not None:
        prev, *rest = rest
    z_out, xbuf, ybuf, wbuf, zbuf, sem_x, sem_y, sem_w, sem_g, sem_z = rest

    def fetch(g, go):
        if own_only:
            return
        slot, low = first_slot(tab, g), tab[g * 8 + 1]
        when_copy(slot >= 0, recv.at[jnp.maximum(slot, 0)], xbuf.at[g], sem_x.at[g], go)
        when_copy(two_links(tab, g), recv.at[jnp.maximum(low, 0)], ybuf.at[g], sem_y.at[g], go)
        if go:

            @pl.when(slot < 0)
            def _():
                xbuf[g] = jnp.zeros_like(xbuf[g])

    def fetch_own(step, go):
        group = pl.ds(step * WIDTH, WIDTH)
        copies = [pltpu.make_async_copy(part.at[group], zbuf.at[group], sem_g.at[step])]
        if back is not None:
            copies.append(pltpu.make_async_copy(prev.at[group], wbuf.at[group], sem_w.at[step]))
        for copy in copies:
            copy.start() if go else copy.wait()

    def keep(g):
        return pltpu.make_async_copy(zbuf.at[g], z_out.at[g], sem_z.at[g])

    @pl.loop(0, count // WIDTH)
    def _(step):
        for k in range(WIDTH):
            fetch(step * WIDTH + k, True)
        fetch_own(step, True)

    def linked(group, buf, above):
        both = [weights(wts, g, a) for g, a in zip(group, above)]
        values = [(0.0, 0.0) if own_only else (buf[g, 0], buf[g, 1]) for g in group]
        if back is not None:
            own = [(wbuf[g, 0], wbuf[g, 1]) for g in group]
            terms = product(
                left[...], right[...], own, [b[1][0] for b in both], [b[1][1] for b in both]
            )
            values = [
                tuple(back * (v + t) for v, t in zip(value, term))
                for value, term in zip(values, terms)
            ]
        return product(
            left[...], right[...], values, [b[0][0] for b in both], [b[0][1] for b in both]
        )

    @pl.loop(0, count // WIDTH)
    def _(step):
        group = [step * WIDTH + k for k in range(WIDTH)]
        for g in group:
            fetch(g, False)
        fetch_own(step, False)
        above = [tab[g * 8] >= 0 for g in group]
        for g, term in zip(group, linked(group, xbuf, above)):
            for p in range(2):
                if last:
                    zbuf[g, p] = zbuf[g, p] + scale * term[p]
                else:
                    zbuf[g, p] = scale * (zbuf[g, p] + term[p])
        for g in group:

            @pl.when(two_links(tab, g))
            def _():
                (term,) = linked([g], ybuf, [False])
                for p in range(2):
                    zbuf[g, p] = zbuf[g, p] + scale * term[p]

        for g in group:
            keep(g).start()

    @pl.loop(0, count)
    def _(g):
        keep(g).wait()


def row_part(tab, wts, token, recv, part, prev, left, right, scale, back, last, own_only=False):
    count, _, n, _ = part.shape
    out = jax.ShapeDtypeStruct(part.shape, f32) if last else pltpu.HBM(part.shape, f32)
    olds = [] if back is None else in_hbm(prev)
    return pl.pallas_call(
        functools.partial(row_kernel, scale=scale, back=back, last=last, own_only=own_only),
        out_shape=out,
        in_specs=[SMEM, SMEM, SMEM, HBM, HBM, VMEM, VMEM] + [HBM] * len(olds),
        out_specs=HBM,
        scratch_shapes=[pltpu.VMEM((count, 2, n, n), f32)] * 4
        + [pltpu.SemaphoreType.DMA((count,))] * 5,
        compiler_params=pltpu.CompilerParams(vmem_limit_bytes=LIMIT),
        cost_estimate=pl.CostEstimate(
            flops=count * 64 * n * n * n, bytes_accessed=10 << 20, transcendentals=0
        ),
        name="row_part",
    )(tab, wts, token, *in_hbm(recv, part), left, right, *olds)


def local(
    densities, hamiltonian, couplings, decay_rates, correlation, upper_link, lower_link, occupation
):
    count, _, n, _ = densities.shape
    along_y, along_x = lax.axis_size("gy"), lax.axis_size("gx")
    index_x, index_y = lax.axis_index("gx"), lax.axis_index("gy")
    own = index_x * along_y + index_y
    missing = count * along_y * along_x

    row_send = pl.pallas_call(
        functools.partial(pack_rows_kernel, missing=missing, bath=2),
        out_shape=pltpu.HBM((along_y, 2, n, n), f32),
        in_specs=[SMEM, SMEM, HBM],
        out_specs=HBM,
        scratch_shapes=[pltpu.VMEM((count, 2, n, n), f32)]
        + [pltpu.SemaphoreType.DMA((count,))] * 3,
        name="pack_rows",
    )(upper_link.T, lower_link.T, densities)

    links = jnp.stack([upper_link, lower_link], axis=2)
    live = links < missing
    near = jnp.where(live[:, 0:2], links[:, 0:2] - own * count, -1).reshape(count, 4)
    rows = jnp.where(live[:, 2], (links[:, 2] // count) % along_y, -1)

    targets, usable = links[:, 3].reshape(-1), live[:, 3].reshape(-1)
    sources = jnp.repeat(jnp.arange(count, dtype=jnp.int32), 2)
    relative = (targets // count // along_y - index_x) % along_x
    same = usable[:, None] & usable[None, :] & (relative[:, None] == relative[None, :])
    start = (relative - 1) * XCAP
    recv_slot = start + jnp.any(same & (targets[None, :] < targets[:, None]), axis=1)
    send_slot = start + jnp.any(same & (sources[None, :] < sources[:, None]), axis=1)
    recv_slot = jnp.where(usable, recv_slot, -1).reshape(count, 2)
    hit = (send_slot[None, :] == jnp.arange(6, dtype=jnp.int32)[:, None]) & usable[None, :]
    ctab = jnp.max(jnp.where(hit, sources[None, :], -1), axis=1)
    tab = jnp.concatenate([rows, near, recv_slot], axis=1).reshape(-1).astype(jnp.int32)

    level = occupation.astype(f32)
    damping = jnp.sum(level * decay_rates[None, :], axis=1, keepdims=True)
    pairs = (level[:, :, None] * correlation.T[None, :, :]).reshape(count, 8)
    third = jnp.broadcast_to(correlation[:, 2][None, :], (count, 2))
    wts = jnp.concatenate([pairs, damping, third], axis=1).reshape(-1)

    mats = lambda rows, cols: jax.ShapeDtypeStruct((rows, cols), bf16)
    left, right, row_left, row_right = pl.pallas_call(
        prepare_kernel,
        out_shape=[mats(2 * n, 10 * n), mats(10 * n, 2 * n), mats(2 * n, 2 * n), mats(2 * n, 2 * n)],
        in_specs=[VMEM, VMEM],
        out_specs=[VMEM] * 4,
        name="prepare",
    )(hamiltonian, couplings)

    exchange = lambda a: lax.all_to_all(a, "gy", split_axis=0, concat_axis=0, tiled=True)
    states, acc, parts = [densities], None, None
    token = jnp.zeros((1,), jnp.int32)
    recv = exchange(row_send)
    for level in range(4):
        z, last = states[level], level == 3
        col_send = pack_columns(ctab, z)
        arrived = [
            lax.ppermute(col_send[s - 1], "gx", [(x, (x + s) % along_x) for x in range(along_x)])
            for s in range(1, along_x)
        ]
        scale = step_size / (level + 1)
        back = step_size / level if level else None
        prev = states[level - 1] if level else None
        mats = (row_left, row_right)
        if last:
            acc = row_part(tab, wts, token, prev, acc, prev, *mats, scale, back, True, own_only=True)
            scale_row, back = scale * back, None
        else:
            scale_row = scale
        parts = local_part(
            tab, wts, z, arrived[::-1], left, right, acc, along_y, scale if last else None
        )
        acc = densities if level == 0 else None if last else parts[2]
        if not last:
            slots, token = fix_slots(tab, wts, recv, parts[0], parts[1], prev, *mats, back)
            following = exchange(slots)
        new = row_part(tab, wts, token, recv, parts[0], prev, *mats, scale_row, back, last)
        if last:
            return new
        states.append(new)
        recv = following


def solution(mesh):
    return jax.shard_map(
        local,
        mesh=mesh,
        in_specs=(
            P(("gx", "gy"), None, None, None),
            P(),
            P(),
            P(),
            P(),
            P(("gx", "gy"), None),
            P(("gx", "gy"), None),
            P(("gx", "gy"), None),
        ),
        out_specs=P(("gx", "gy"), None, None, None),
        check_vma=False,
    )
```
